512 devices in a mesh: rows: 128 (over y_hi, z, x), feat: 4 (over y_lo, core).
Axes of the slice: x: 4, y: 4 (y_hi: 2, y_lo: 2; y = y_hi * 2 + y_lo), z: 16, core: 2. Of those that a mesh axis runs over, the one named last changes fastest.
Arguments:
- edge_feats: bfloat16 [131072, 256], P(('rows', 'feat')), may hold values from -6 to 6
- edge_owner: int32 [131072, 1], P(('rows', 'feat')), may hold values from 0 to 127; in each aligned block of 256 rows (0 to 255, 256 to 511, ...) at most 4 rows name the same one
- src_local: int32 [131072], P(('rows', 'feat')), may hold values from 0 to 63
- band_slot: int32 [131072], P(('rows', 'feat')), may hold values from 0 to 8
- dst_local: int32 [131072], P(('rows', 'feat')), may hold values from 0 to 7
- w_first: bfloat16 [256, 256], replicated, may hold values from -0.375 to 0.375
- w_second: bfloat16 [256, 256], replicated, may hold values from -0.375 to 0.375
- w_third: bfloat16 [256, 256], replicated, may hold values from -0.375 to 0.375
Outputs:
- density: float32 [1024, 9, 128, 128], P('rows', None, 'feat')
The draws below stay inside these ranges and needn't reach their ends.
Inputs may be any that keep to these rules, and one draw needn't show every extreme that they name: `edge_owner`: among the 256 edges of one device (aligned blocks of rows), no index of rows is named more than 4 times, a bound that some block reaches.
All inputs are finite; a program needn't handle non-finite values.
Results may differ from the reference program's by a relative error of at most 0.0014.
Values sent between devices are 32-bit elements; how exact they have to be, the bound alone decides.
No kernel may reach another device: no remote copies, remote signals or barrier semaphores. Data moves between devices by JAX's collectives and lax.ppermute only.
A program may use at most 64 MiB of HBM per device.

```python
import math
import jax
import jax.numpy as jnp
import numpy as np
from jax import lax

F = 256
BLOCK = 16
TILE = 128
BAND = 9
TILE_DEV = 8
EDGE_DEV = 256
CAP = 4
BPT = 8
TILES = 1024
EDGES = 131072
N_ROWS = 128
N_FEAT = 4


def with_ends(drawn, key, low, largest):
    dims = drawn.shape
    place = [jax.random.randint(jax.random.fold_in(key, axis), (), 0, dims[axis]) for axis in range(len(dims))]
    drawn = drawn.at[tuple(place)].set(low)
    longest = dims.index(max(dims))
    place[longest] = (place[longest] + 1) % dims[longest]
    return drawn.at[tuple(place)].set(largest)


def shard_levels(rng, dims, split, low, largest):
    def one(axis_at, shards_of):
        draws = jax.random.uniform(jax.random.fold_in(jax.random.fold_in(rng, 6), axis_at), (shards_of,), jnp.float32, low / len(split), largest / len(split))
        return jnp.repeat(jnp.exp(draws), dims[axis_at] // shards_of).reshape((-1,) + (1,) * (len(dims) - axis_at - 1))

    factor_of = one(*split[0])
    for cut in split[1:]:
        factor_of = factor_of * one(*cut)
    return factor_of


def routed_block(rng, own, number, rows, amount, top, limit, lean):
    sequence = jax.random.permutation(rng, amount)
    heavy_load, usual = shares(amount, rows * top, limit, lean, True), shares(amount, rows * top, limit, lean, False)
    places = jnp.arange(amount)

    def named(tallies, rotation):
        used = int((tallies > 0).sum())
        fixed = max(1, used // 4)
        moved = fixed + (places - fixed + rotation * (used - fixed)) % max(1, amount - fixed)
        return jnp.zeros((amount,), jnp.int32).at[sequence[jnp.where(places < fixed, places, moved)]].set(jnp.asarray(tallies, jnp.int32))

    tallies = jnp.where(number % 4 == 0, named(heavy_load, number // 4), named(usual, number - number // 4 - 1))
    mixed = jax.random.permutation(jax.random.fold_in(own, 3), amount)
    source_of, receiver = mixed[0:amount // 2 * 2:2], mixed[1:amount // 2 * 2:2]
    room = jnp.minimum(tallies[source_of] - 1, limit - tallies[receiver]) // 2
    room = jnp.where((source_of == sequence[0]) | (receiver == sequence[0]) | (tallies[receiver] == 0), 0, jnp.maximum(room, 0))
    moved = jax.random.randint(jax.random.fold_in(own, 4), (amount // 2,), 0, 1 << 20) % (room + 1)
    tallies = tallies.at[source_of].add(-moved).at[receiver].add(moved)
    items = jnp.searchsorted(jnp.cumsum(tallies), jnp.arange(rows * top), side="right").astype(jnp.int32)
    listing = items.reshape(top, rows).T
    listing = listing[jax.random.permutation(jax.random.fold_in(own, 1), rows)]
    rotation = jax.random.randint(jax.random.fold_in(own, 2), (rows, 1), 0, top)
    return jnp.take_along_axis(listing, (jnp.arange(top)[None, :] + rotation) % top, axis=1)


def shares(count, total, reach, slope, full):
    loads = [(1 << 20) // math.isqrt(rank ** slope) + 1 for rank in range(1, count + 1)]
    largest = reach if full else min(reach, max(-(-total // count), total * loads[0] // sum(loads)))
    least = 1 if total - largest >= count - 1 else 0
    counts, rest = [largest] + [least] * (count - 1), total - largest - least * (count - 1)
    while rest > 0:
        movable = [i for i in range(1, count) if counts[i] < largest] or [i for i in range(1, count) if counts[i] < reach]
        pool, remaining = sum([loads[i] for i in movable]), rest
        for i in movable:
            extra = min(reach - counts[i], max(1, remaining * loads[i] // pool), rest)
            counts[i] = counts[i] + extra
            rest = rest - extra
    return np.array(counts)


def normal_values(rng, shape, spread, reach, pieces=(), kind=jnp.bfloat16):
    result = spread * jax.random.normal(rng, shape, jnp.float32)
    if pieces:
        result = result * shard_levels(rng, shape, pieces, -0.22, 0.18)
    return jnp.clip(result, -reach, reach).astype(kind)


def setup_inputs(seed: int = 0) -> dict:
    keys = jax.random.split(jax.random.key(seed), 9)
    edge_feats = normal_values(keys[0], (EDGES, F), 1.0, 6.0, ((0, 512),))
    edge_owner_keys = jax.random.split(jax.random.fold_in(keys[1], 1), EDGES // EDGE_DEV)
    edge_owner_turns = jax.random.permutation(jax.random.fold_in(keys[1], 3), EDGES // EDGE_DEV)
    edge_owner = jax.vmap(lambda own, number: routed_block(jax.random.fold_in(keys[1], 2), own, number, EDGE_DEV, N_ROWS, 1, CAP, 2))(edge_owner_keys, edge_owner_turns).reshape((EDGES, 1))
    src_local = with_ends(jax.random.randint(keys[2], (EDGES,), 0, TILE_DEV * BPT), jax.random.fold_in(keys[2], 1), 0, (TILE_DEV * BPT) - 1).astype(jnp.int32)
    band_slot = with_ends(jax.random.randint(keys[3], (EDGES,), 0, BAND), jax.random.fold_in(keys[3], 1), 0, BAND - 1).astype(jnp.int32)
    dst_local = with_ends(jax.random.randint(keys[4], (EDGES,), 0, BPT), jax.random.fold_in(keys[4], 1), 0, BPT - 1).astype(jnp.int32)
    w_first = normal_values(keys[5], (F, F), F ** -0.5, 0.375)
    w_second = normal_values(keys[6], (F, F), F ** -0.5, 0.375)
    w_third = normal_values(keys[7], (F, BLOCK * BLOCK), F ** -0.5, 0.375)
    return dict(edge_feats=edge_feats, edge_owner=edge_owner, src_local=src_local, band_slot=band_slot, dst_local=dst_local, w_first=w_first, w_second=w_second, w_third=w_third)


def edge_values(edge_feats, w_first, w_second, w_third):
    hidden_one = jax.nn.silu(jnp.dot(edge_feats, w_first, preferred_element_type=jnp.float32)).astype(jnp.bfloat16)
    hidden_two = jax.nn.silu(jnp.dot(hidden_one, w_second, preferred_element_type=jnp.float32)).astype(jnp.bfloat16)
    return jnp.dot(hidden_two, w_third, preferred_element_type=jnp.float32)

def band_product(left_band, right_band):
    half_band = BAND // 2
    summed = jnp.zeros(left_band.shape, jnp.float32)
    for offset in range(BAND):
        shifted = jnp.roll(right_band, -(offset - half_band), axis=0)
        lower_slot = max(0, offset - half_band)
        upper_slot = min(BAND, offset + half_band + 1)
        product = jnp.einsum('irm,icmk->icrk', left_band[:, offset], shifted[:, lower_slot - offset + half_band:upper_slot - offset + half_band], precision=lax.Precision.HIGHEST)
        summed = summed.at[:, lower_slot:upper_slot].add(product)
    return summed

def reference(edge_feats, edge_owner, src_local, band_slot, dst_local, w_first, w_second, w_third):
    group_cols = BLOCK // N_FEAT
    col_width = TILE // N_FEAT
    blocks_tile = TILE // BLOCK
    half_band = BAND // 2
    values = edge_values(edge_feats, w_first, w_second, w_third)
    entries = jnp.arange(BLOCK * BLOCK, dtype=jnp.int32)
    group_index = entries // (BLOCK * group_cols)
    component = entries // group_cols % BLOCK
    unit_col = entries % group_cols
    tile_row = edge_owner[:, 0] * TILE_DEV + src_local // blocks_tile
    src_block = src_local % blocks_tile
    row_pos = (component // group_cols)[None, :] * col_width + src_block[:, None] * group_cols + (component % group_cols)[None, :]
    col_pos = group_index[None, :] * col_width + dst_local[:, None] * group_cols + unit_col[None, :]
    flat_index = ((tile_row * BAND + band_slot)[:, None] * TILE + row_pos) * TILE + col_pos
    hamil = jnp.zeros((TILES * BAND * TILE * TILE,), jnp.float32)
    hamil = hamil.at[flat_index.reshape(-1)].add(values.reshape(-1)).reshape(TILES, BAND, TILE, TILE)
    partner = jnp.stack([jnp.roll(hamil[:, BAND - 1 - slot_index], -(slot_index - half_band), axis=0) for slot_index in range(BAND)], axis=1)
    degree = N_FEAT * EDGE_DEV / (TILE_DEV * blocks_tile)
    gamma = 0.5 / math.sqrt(2.0 * BLOCK * degree)
    start = 0.5 * gamma * (hamil + jnp.swapaxes(partner, 2, 3))
    start = start.at[:, half_band].add(0.5 * jnp.eye(TILE, dtype=jnp.float32))
    squared = band_product(start, start)
    purified = 2.0 * squared - band_product(squared, squared)
    return jnp.swapaxes(purified, 2, 3)
```

```python
import functools
import math

import jax
import jax.numpy as jnp
from jax import lax
from jax.experimental import pallas as pl
from jax.experimental.pallas import tpu as pltpu
from jax.sharding import PartitionSpec as P

BLOCK = 16
TILE = 128
BAND = 9
HALF = BAND // 2
TILE_DEV = 8
BPT = TILE // BLOCK
F = 256
CAP = 4
PEERS = 128
RECORD_ROWS = 2 * CAP + 1
FEAT = 4
COLS = TILE // FEAT
BF = jnp.bfloat16
F32 = jnp.float32


def dot(a, b):
    return jnp.dot(a, b, preferred_element_type=F32)


def dot_t(a, b):
    return lax.dot_general(a, b, (((1,), (1,)), ((), ())), preferred_element_type=F32)


def pieces(x):
    high = x.astype(BF)
    return high, (x - high.astype(F32)).astype(BF)


def pack_kernel(feats, owner, src, slot, dst, w_first, w_second, out):
    edges = feats.shape[0]
    hidden = jax.nn.silu(dot(feats[...], w_first[...])).astype(BF)
    hidden = jax.nn.silu(dot(hidden, w_second[...])).astype(BF)
    named = lax.broadcasted_iota(jnp.int32, (PEERS, edges), 0) == owner[...]
    onehot = named.astype(F32)
    before = lax.broadcasted_iota(jnp.int32, (edges, edges), 0) < lax.broadcasted_iota(
        jnp.int32, (edges, edges), 1
    )
    earlier = dot(onehot.astype(BF), before.astype(F32).astype(BF))
    rank = jnp.sum(onehot * earlier, axis=0, keepdims=True)
    src_v, slot_v, dst_v = src[...], slot[...], dst[...]
    tile_code = ((src_v // BPT) * BAND + slot_v).astype(F32)
    block_code = ((src_v % BPT) * BPT + dst_v).astype(F32)
    lane = lax.broadcasted_iota(jnp.int32, (PEERS, TILE), 1)
    codes = jnp.zeros((PEERS, TILE), F32)
    for k in range(CAP):
        chosen = jnp.where(rank == float(k), onehot, 0.0)
        placed = dot(chosen.astype(BF), hidden)
        out[pl.ds(2 * k, PEERS, stride=RECORD_ROWS), :] = placed[:, :TILE]
        out[pl.ds(2 * k + 1, PEERS, stride=RECORD_ROWS), :] = placed[:, TILE:]
        tile_of = jnp.sum(chosen * tile_code, axis=1, keepdims=True)
        block_of = jnp.sum(chosen * block_code, axis=1, keepdims=True)
        codes = codes + jnp.where(lane == k, tile_of, 0.0)
        codes = codes + jnp.where(lane == CAP + k, block_of, 0.0)
    out[pl.ds(2 * CAP, PEERS, stride=RECORD_ROWS), :] = codes


def pack(feats, owner, src, slot, dst, w_first, w_second):
    return pl.pallas_call(
        pack_kernel,
        out_shape=jax.ShapeDtypeStruct((PEERS * RECORD_ROWS, TILE), F32),
        name="pack",
    )(feats, owner, src, slot, dst, w_first, w_second)


ROWS_T = TILE_DEV * BAND * BPT
RECORDS = FEAT * CAP * PEERS


def gather_kernel(scale, b0, b1, b2, b3, w_third, out, hid, code, spread):
    for f, blk in enumerate((b0, b1, b2, b3)):
        codes = jnp.transpose(blk[pl.ds(2 * CAP, PEERS, stride=RECORD_ROWS), :])
        for k in range(CAP):
            at = (f * CAP + k) * PEERS
            for half in range(2):
                hid[at : at + PEERS, half * TILE : (half + 1) * TILE] = blk[
                    pl.ds(2 * k + half, PEERS, stride=RECORD_ROWS), :
                ].astype(BF)
            tile_of = codes[k : k + 1, :].astype(jnp.int32)
            block_of = codes[CAP + k : CAP + k + 1, :].astype(jnp.int32)
            code[0:1, at : at + PEERS] = (
                (block_of % BPT) * ROWS_T + tile_of * BPT + block_of // BPT
            )
    w = w_third[...]

    def place(b, carry):
        base = b * ROWS_T
        spot = lax.broadcasted_iota(jnp.int32, (ROWS_T, RECORDS), 0) + base
        onehot = jnp.where(spot == code[0:1, :], 1.0, 0.0).astype(BF)
        high, low = pieces(dot(onehot, hid[...]))
        spread[b] = (dot(high, w) + dot(low, w)) * scale
        return carry

    lax.fori_loop(0, BPT, place, 0)
    lane = lax.broadcasted_iota(jnp.int32, (BPT, TILE), 1)

    def arrange(t, carry):
        rows = pl.ds(pl.multiple_of(t * BPT, BPT), BPT)
        for half in range(2):
            x = [spread[b, rows, half * TILE : (half + 1) * TILE] for b in range(BPT)]
            for bit in (1, 2, 4):
                shift = 4 * bit
                upper = (lane // shift) % 2 == 1
                for i in range(BPT):
                    if not i & bit:
                        a, c = x[i], x[i | bit]
                        x[i] = jnp.where(upper, pltpu.roll(c, shift, 1), a)
                        x[i | bit] = jnp.where(upper, c, pltpu.roll(a, TILE - shift, 1))
            for q in range(BPT):
                comp = half * BPT + q
                first = (comp // 4) * COLS + comp % 4
                out[t, pl.ds(first, BPT, stride=4), :] = x[q]
        return carry

    lax.fori_loop(0, TILE_DEV * BAND, arrange, 0)


def gather_blocks(scale, blocks, w):
    return pl.pallas_call(
        functools.partial(gather_kernel, scale),
        out_shape=jax.ShapeDtypeStruct((TILE_DEV * BAND, TILE, TILE), F32),
        scratch_shapes=[
            pltpu.VMEM((RECORDS, F), BF),
            pltpu.VMEM((8, RECORDS), jnp.int32),
            pltpu.VMEM((BPT, ROWS_T, F), F32),
        ],
        compiler_params=pltpu.CompilerParams(vmem_limit_bytes=56 * 2**20),
        cost_estimate=pl.CostEstimate(
            flops=2 * BPT * ROWS_T * F * (RECORDS + 2 * F),
            bytes_accessed=7 * 2**20,
            transcendentals=0,
        ),
        name="gather_blocks",
    )(*blocks, w)


PAIR = 2 * TILE
SPAN = 5 * PAIR
INNER = 8


def purify_kernel(group, ham, out, e_hi, e_lo, f_hi, f_lo, g_hi, g_lo):
    zero = jnp.zeros((TILE, TILE), BF)

    def fill(p, carry):
        for par in range(2):
            a = 2 * (p + 2) + par
            rows = slice(par * TILE, (par + 1) * TILE)
            edge = slice(0, TILE) if par else slice(9 * TILE, 10 * TILE)
            e_hi[p, rows, edge] = zero
            e_lo[p, rows, edge] = zero
            for s in range(BAND):
                b = a + s - HALF
                x = ham[a * BAND + s] + jnp.transpose(ham[b * BAND + BAND - 1 - s])
                at = slice((s + par) * TILE, (s + par + 1) * TILE)
                e_hi[p, rows, at], e_lo[p, rows, at] = pieces(x)
        return carry

    lax.fori_loop(0, INNER, fill, 0)

    row_tile = lax.broadcasted_iota(jnp.int32, (PAIR, PAIR), 0) // TILE
    col_tile = lax.broadcasted_iota(jnp.int32, (PAIR, PAIR), 1) // TILE

    def square(p, carry):
        for d in range(3):

            @pl.when(p + d < INNER)
            def _():
                o = p + d
                k = SPAN - d * PAIR
                a_hi, a_lo = e_hi[p, :, d * PAIR :], e_lo[p, :, d * PAIR :]
                b_hi, b_lo = e_hi[o, :, :k], e_lo[o, :, :k]
                at = slice((2 + d) * PAIR, (3 + d) * PAIR)
                x = dot_t(a_hi, b_hi) + (dot_t(a_hi, b_lo) + dot_t(a_lo, b_hi))
                if d == 2:
                    x = jnp.where(col_tile > row_tile, 0.0, x)
                x = x + (e_hi[p, :, at].astype(F32) + e_lo[p, :, at].astype(F32))
                f_hi[p, :, at], f_lo[p, :, at] = pieces(x)
                if d:
                    back = slice((2 - d) * PAIR, (3 - d) * PAIR)
                    f_hi[o, :, back], f_lo[o, :, back] = pieces(jnp.transpose(x))

        return carry

    lax.fori_loop(0, INNER, square, 0)

    mine = pl.multiple_of(group[0] * COLS, COLS)
    g_hi[...] = jnp.zeros_like(g_hi)
    g_lo[...] = jnp.zeros_like(g_lo)
    for p in range(INNER):
        low, high = max(0, p - 2), min(INNER, p + 3)
        source = slice((low - p + 2) * PAIR, (high - p + 2) * PAIR)
        for par in range(2):
            rows = slice((2 * p + par) * COLS, (2 * p + par + 1) * COLS)
            from_rows = pl.ds(par * TILE + mine, COLS)
            for g_ref, f_ref in ((g_hi, f_hi), (g_lo, f_lo)):
                g_ref[rows, low * PAIR : high * PAIR] = f_ref[p, from_rows, source]

    diagonal = lax.broadcasted_iota(jnp.int32, (COLS, TILE), 0) + mine == (
        lax.broadcasted_iota(jnp.int32, (COLS, TILE), 1)
    )
    diagonal = jnp.where(diagonal, 7.0 / 16.0, 0.0)
    for m in range(4):
        p = m + 2
        rows = slice(m * 2 * COLS, (m + 5) * 2 * COLS)
        span = slice(m * PAIR, (m + 5) * PAIR)
        own = slice(p * PAIR, (p + 1) * PAIR)
        l_hi, l_lo, r_hi, r_lo = g_hi[rows, span], g_lo[rows, span], f_hi[p], f_lo[p]
        x = dot_t(l_hi, r_hi) + (dot_t(l_hi, r_lo) + dot_t(l_lo, r_hi))
        x = 1.5 * (g_hi[rows, own].astype(F32) + g_lo[rows, own].astype(F32)) - x
        for par in range(2):
            for s in range(BAND):
                y = x[(s + par) * COLS : (s + par + 1) * COLS, par * TILE : (par + 1) * TILE]
                if s == HALF:
                    y = y + diagonal
                out[2 * m + par, s] = y


def purify(group, ham):
    return pl.pallas_call(
        purify_kernel,
        out_shape=jax.ShapeDtypeStruct((TILE_DEV, BAND, COLS, TILE), F32),
        in_specs=[
            pl.BlockSpec(memory_space=pltpu.SMEM),
            pl.BlockSpec(memory_space=pltpu.VMEM),
        ],
        scratch_shapes=[pltpu.VMEM((INNER, PAIR, SPAN), BF)] * 4
        + [pltpu.VMEM((2 * INNER * COLS, INNER * PAIR), BF)] * 2,
        compiler_params=pltpu.CompilerParams(vmem_limit_bytes=60 * 2**20),
        name="purify",
    )(group, ham)


def swap(x, axis_bit):
    pairs = [(r * FEAT + g, r * FEAT + (g ^ axis_bit)) for r in range(PEERS) for g in range(FEAT)]
    return lax.ppermute(x, ("rows", "feat"), pairs)


def shift(x, step):
    pairs = [(r, (r + step) % PEERS) for r in range(PEERS)]
    return lax.ppermute(x, "rows", pairs)


def local(edge_feats, edge_owner, src_local, band_slot, dst_local, w_first, w_second, w_third):
    edges = edge_feats.shape[0]
    row = lambda x: x.reshape(1, edges)
    sent = pack(
        edge_feats, row(edge_owner), row(src_local), row(band_slot), row(dst_local),
        w_first, w_second,
    )
    got = lax.all_to_all(
        sent.reshape(PEERS, 1, RECORD_ROWS * TILE), "rows", split_axis=0, concat_axis=0, tiled=True
    )
    got = got.reshape(PEERS * RECORD_ROWS, TILE)
    half_scale = 0.25 / math.sqrt(2.0 * BLOCK * FEAT * edges / (TILE_DEV * BPT))
    w = w_third.reshape(F, FEAT, 2, BPT, 4).transpose(0, 2, 1, 3, 4).reshape(F, F)
    across = swap(got, 2)
    held = [
        (got, across),
        (shift(got, 1), shift(across, 1)),
        (shift(got, -1), shift(across, -1)),
    ]
    own, before, after = [
        gather_blocks(half_scale, (a, b, swap(a, 1), swap(b, 1)), w) for a, b in held
    ]
    ham = jnp.concatenate([before, own, after], axis=0)
    return purify(lax.axis_index("feat").astype(jnp.int32).reshape(1), ham)


def solution(mesh):
    in_specs = (
        P(("rows", "feat"), None),
        P(("rows", "feat"), None),
        P(("rows", "feat")),
        P(("rows", "feat")),
        P(("rows", "feat")),
        P(),
        P(),
        P(),
    )
    out_specs = P("rows", None, "feat", None)
    return jax.shard_map(local, mesh=mesh, in_specs=in_specs, out_specs=out_specs, check_vma=False)
```

```python
import functools
import math

import jax
import jax.numpy as jnp
from jax import lax
from jax.experimental import pallas as pl
from jax.experimental.pallas import tpu as pltpu
from jax.sharding import PartitionSpec as P

BLOCK = 16
TILE = 128
BAND = 9
HALF = BAND // 2
TILE_DEV = 8
BPT = TILE // BLOCK
F = 256
CAP = 4
PEERS = 128
RECORD_ROWS = 2 * CAP + 1
FEAT = 4
COLS = TILE // FEAT
BF = jnp.bfloat16
F32 = jnp.float32


def dot(a, b):
    return jnp.dot(a, b, preferred_element_type=F32)


def dot_t(a, b):
    return lax.dot_general(a, b, (((1,), (1,)), ((), ())), preferred_element_type=F32)


def pieces(x):
    high = x.astype(BF)
    return high, (x - high.astype(F32)).astype(BF)


def pack_kernel(feats, owner, src, slot, dst, w_first, w_second, out):
    edges = feats.shape[0]
    hidden = jax.nn.silu(dot(feats[...], w_first[...])).astype(BF)
    hidden = jax.nn.silu(dot(hidden, w_second[...])).astype(BF)
    named = lax.broadcasted_iota(jnp.int32, (PEERS, edges), 0) == owner[...]
    onehot = named.astype(F32)
    before = lax.broadcasted_iota(jnp.int32, (edges, edges), 0) < lax.broadcasted_iota(
        jnp.int32, (edges, edges), 1
    )
    earlier = dot(onehot.astype(BF), before.astype(F32).astype(BF))
    rank = jnp.sum(onehot * earlier, axis=0, keepdims=True)
    src_v, slot_v, dst_v = src[...], slot[...], dst[...]
    tile_code = ((src_v // BPT) * BAND + slot_v).astype(F32)
    block_code = ((src_v % BPT) * BPT + dst_v).astype(F32)
    lane = lax.broadcasted_iota(jnp.int32, (PEERS, TILE), 1)
    codes = jnp.zeros((PEERS, TILE), F32)
    for k in range(CAP):
        chosen = jnp.where(rank == float(k), onehot, 0.0)
        placed = dot(chosen.astype(BF), hidden)
        out[pl.ds(2 * k, PEERS, stride=RECORD_ROWS), :] = placed[:, :TILE]
        out[pl.ds(2 * k + 1, PEERS, stride=RECORD_ROWS), :] = placed[:, TILE:]
        tile_of = jnp.sum(chosen * tile_code, axis=1, keepdims=True)
        block_of = jnp.sum(chosen * block_code, axis=1, keepdims=True)
        codes = codes + jnp.where(lane == k, tile_of, 0.0)
        codes = codes + jnp.where(lane == CAP + k, block_of, 0.0)
    out[pl.ds(2 * CAP, PEERS, stride=RECORD_ROWS), :] = codes


def pack(feats, owner, src, slot, dst, w_first, w_second):
    return pl.pallas_call(
        pack_kernel,
        out_shape=jax.ShapeDtypeStruct((PEERS * RECORD_ROWS, TILE), F32),
        name="pack",
    )(feats, owner, src, slot, dst, w_first, w_second)


RECORDS = FEAT * CAP * PEERS
OUTER = 4 * BAND + 10


def kept_tile(side, i, s):
    if side == 0:
        return i * BAND + s
    if side < 0:
        inner, outer = i - 4, 36 + i * (i + 1) // 2 + s - (8 - i)
        return jnp.where(i >= 4, inner * BAND + s, jnp.where(s >= 8 - i, outer, -1))
    m = i - 4
    outer = 36 + m * (9 - m) // 2 + s
    return jnp.where(i < 4, i * BAND + s, jnp.where(s <= 3 - m, outer, -1))


def gather_kernel(scale, side, b0, b1, b2, b3, w_third, out, hid, code, spread):
    tiles = out.shape[0]
    rows_t = tiles * BPT
    for f, blk in enumerate((b0, b1, b2, b3)):
        codes = jnp.transpose(blk[pl.ds(2 * CAP, PEERS, stride=RECORD_ROWS), :]).astype(jnp.int32)
        for k in range(CAP):
            at = (f * CAP + k) * PEERS
            for half in range(2):
                hid[at : at + PEERS, half * TILE : (half + 1) * TILE] = blk[
                    pl.ds(2 * k + half, PEERS, stride=RECORD_ROWS), :
                ].astype(BF)
            tile_of, block_of = codes[k : k + 1, :], codes[CAP + k : CAP + k + 1, :]
            tile_of = kept_tile(side, tile_of // BAND, tile_of % BAND)
            place_of = (block_of % BPT) * rows_t + tile_of * BPT + block_of // BPT
            code[0:1, at : at + PEERS] = jnp.where(tile_of >= 0, place_of, -1)
    w = w_third[...].astype(F32)
    w = [
        jnp.concatenate(
            [w[:, g * 64 + h * COLS : g * 64 + (h + 1) * COLS] for g in range(FEAT)], axis=1
        )
        for h in range(2)
    ]

    def place(b, carry):
        turned = [pltpu.roll(x, 4 * b, 1).astype(BF) for x in w]
        spot = lax.broadcasted_iota(jnp.int32, (rows_t, RECORDS), 0) + b * rows_t
        onehot = jnp.where(spot == code[0:1, :], 1.0, 0.0).astype(BF)
        high, low = pieces(dot(onehot, hid[...]))
        turned = jnp.concatenate(turned, axis=1)
        spread[b] = (dot(high, turned) + dot(low, turned)) * scale
        return carry

    lax.fori_loop(0, BPT, place, 0)
    turn = (lax.broadcasted_iota(jnp.int32, (BPT, TILE), 1) // 4) % BPT

    def arrange(step, carry):
        for t in (2 * step, 2 * step + 1):
            rows = pl.ds(pl.multiple_of(t * BPT, BPT), BPT)
            for half in range(2):
                x = [
                    spread[(BPT - j) % BPT, rows, half * TILE : (half + 1) * TILE]
                    for j in range(BPT)
                ]
                for bit in (1, 2, 4):
                    moved = (turn // bit) % 2 == 1
                    x = [jnp.where(moved, x[(j - bit) % BPT], x[j]) for j in range(BPT)]
                for q in range(BPT):
                    comp = half * BPT + q
                    first = (comp // 4) * COLS + comp % 4
                    y = pltpu.roll(x[q], TILE - 4 * q, 1) if q else x[q]
                    out[t, pl.ds(first, BPT, stride=4), :] = y
        return carry

    lax.fori_loop(0, tiles // 2, arrange, 0)


def gather_blocks(scale, side, blocks, w):
    tiles = OUTER if side else TILE_DEV * BAND
    rows_t = tiles * BPT
    return pl.pallas_call(
        functools.partial(gather_kernel, scale, side),
        out_shape=jax.ShapeDtypeStruct((tiles, TILE, TILE), F32),
        scratch_shapes=[
            pltpu.VMEM((RECORDS, F), BF),
            pltpu.VMEM((8, RECORDS), jnp.int32),
            pltpu.VMEM((BPT, rows_t, F), F32),
        ],
        compiler_params=pltpu.CompilerParams(vmem_limit_bytes=56 * 2**20),
        cost_estimate=pl.CostEstimate(
            flops=2 * BPT * rows_t * F * (RECORDS + 2 * F),
            bytes_accessed=7 * 2**20,
            transcendentals=0,
        ),
        name="gather_blocks",
    )(*blocks, w)


PAIR = 2 * TILE
SPAN = 5 * PAIR
INNER = 8
SLICE = 2 * COLS


def purify_kernel(group, before, own, after, out, e_hi, e_lo, f_hi, f_lo, g_hi, g_lo, s_hi, s_lo):
    def tile(a, s):
        if a < 4:
            return before[36 + a * (a + 1) // 2 + s - (8 - a)]
        if a < 8:
            return before[(a - 4) * BAND + s]
        if a < 16:
            return own[(a - 8) * BAND + s]
        if a < 20:
            return after[(a - 16) * BAND + s]
        return after[36 + (a - 20) * (29 - a) // 2 + s]

    zero = jnp.zeros((TILE, TILE), BF)
    for p in range(INNER):
        for par in range(2):
            a = 2 * (p + 2) + par
            rows = slice(par * TILE, (par + 1) * TILE)
            edge = slice(0, TILE) if par else slice(9 * TILE, 10 * TILE)
            e_hi[p, rows, edge] = zero
            e_lo[p, rows, edge] = zero
            for s in range(BAND):
                x = tile(a, s) + jnp.transpose(tile(a + s - HALF, BAND - 1 - s))
                at = slice((s + par) * TILE, (s + par + 1) * TILE)
                e_hi[p, rows, at], e_lo[p, rows, at] = pieces(x)

    mine = pl.multiple_of(group[0] * COLS, COLS)
    row_tile = lax.broadcasted_iota(jnp.int32, (PAIR, PAIR), 0) // TILE
    col_tile = lax.broadcasted_iota(jnp.int32, (PAIR, PAIR), 1) // TILE

    def product(a_hi, a_lo, b_hi, b_lo):
        return dot_t(a_hi, b_hi) + (dot_t(a_hi, b_lo) + dot_t(a_lo, b_hi))

    def square(d, p, carry):
        o = p + d
        k = SPAN - d * PAIR
        at = slice((2 + d) * PAIR, (3 + d) * PAIR)
        x = product(e_hi[p, :, d * PAIR :], e_lo[p, :, d * PAIR :], e_hi[o, :, :k], e_lo[o, :, :k])
        if d == 2:
            x = jnp.where(col_tile > row_tile, 0.0, x)
        x = x + (e_hi[p, :, at].astype(F32) + e_lo[p, :, at].astype(F32))
        f_hi[p, :, at], f_lo[p, :, at] = pieces(x)
        if d:
            back = slice((2 - d) * PAIR, (3 - d) * PAIR)
            f_hi[o, :, back], f_lo[o, :, back] = pieces(jnp.transpose(x))
        return carry

    for d, first in ((0, 2), (1, 1), (2, 0)):
        lax.fori_loop(first, 6, functools.partial(square, d), 0)

    g_hi[...] = jnp.zeros_like(g_hi)
    g_lo[...] = jnp.zeros_like(g_lo)
    for p in range(INNER):
        rows = slice(p * SLICE, (p + 1) * SLICE)
        outside = (0, 1) if p < 2 else (6, 7) if p > 5 else ()
        others = [o for o in range(max(0, p - 2), min(INNER, p + 3)) if o not in outside]
        low, high = others[0], others[-1] + 1
        source = slice((low - p + 2) * PAIR, (high - p + 2) * PAIR)
        for par in range(2):
            from_rows = pl.ds(par * TILE + mine, COLS)
            to_rows = slice(p * SLICE + par * COLS, p * SLICE + (par + 1) * COLS)
            for g_ref, f_ref in ((g_hi, f_hi), (g_lo, f_lo)):
                g_ref[to_rows, low * PAIR : high * PAIR] = f_ref[p, from_rows, source]
            if outside:
                for s_ref, e_ref in ((s_hi, e_hi), (s_lo, e_lo)):
                    s_ref[par * COLS : (par + 1) * COLS, :] = e_ref[p, from_rows, :]
        for o in outside:
            left, right = max(0, o - p) * PAIR, max(0, p - o) * PAIR
            k = SPAN - abs(o - p) * PAIR
            x = product(
                s_hi[:, left : left + k], s_lo[:, left : left + k],
                e_hi[o, :, right : right + k], e_lo[o, :, right : right + k],
            )
            at = slice((o - p + 2) * PAIR, (o - p + 3) * PAIR)
            x = x + (s_hi[:, at].astype(F32) + s_lo[:, at].astype(F32))
            g_hi[rows, o * PAIR : (o + 1) * PAIR], g_lo[rows, o * PAIR : (o + 1) * PAIR] = pieces(x)

    diagonal = lax.broadcasted_iota(jnp.int32, (COLS, TILE), 0) + mine == (
        lax.broadcasted_iota(jnp.int32, (COLS, TILE), 1)
    )
    diagonal = jnp.where(diagonal, 7.0 / 16.0, 0.0)
    for m in range(4):
        p = m + 2
        rows = slice(m * SLICE, (m + 5) * SLICE)
        span = slice(m * PAIR, (m + 5) * PAIR)
        at = slice(p * PAIR, (p + 1) * PAIR)
        x = product(g_hi[rows, span], g_lo[rows, span], f_hi[p], f_lo[p])
        x = 1.5 * (g_hi[rows, at].astype(F32) + g_lo[rows, at].astype(F32)) - x
        for par in range(2):
            for s in range(BAND):
                y = x[(s + par) * COLS : (s + par + 1) * COLS, par * TILE : (par + 1) * TILE]
                if s == HALF:
                    y = y + diagonal
                out[2 * m + par, s] = y


def purify(group, before, own, after):
    return pl.pallas_call(
        purify_kernel,
        out_shape=jax.ShapeDtypeStruct((TILE_DEV, BAND, COLS, TILE), F32),
        in_specs=[pl.BlockSpec(memory_space=pltpu.SMEM)]
        + [pl.BlockSpec(memory_space=pltpu.VMEM)] * 3,
        scratch_shapes=[pltpu.VMEM((INNER, PAIR, SPAN), BF)] * 4
        + [pltpu.VMEM((INNER * SLICE, INNER * PAIR), BF)] * 2
        + [pltpu.VMEM((SLICE, SPAN), BF)] * 2,
        compiler_params=pltpu.CompilerParams(vmem_limit_bytes=60 * 2**20),
        name="purify",
    )(group, before, own, after)


def swap(x, axis_bit):
    pairs = [(r * FEAT + g, r * FEAT + (g ^ axis_bit)) for r in range(PEERS) for g in range(FEAT)]
    return lax.ppermute(x, ("rows", "feat"), pairs)


def shift(x, step):
    pairs = [(r, (r + step) % PEERS) for r in range(PEERS)]
    return lax.ppermute(x, "rows", pairs)


def local(edge_feats, edge_owner, src_local, band_slot, dst_local, w_first, w_second, w_third):
    edges = edge_feats.shape[0]
    row = lambda x: x.reshape(1, edges)
    sent = pack(
        edge_feats, row(edge_owner), row(src_local), row(band_slot), row(dst_local),
        w_first, w_second,
    )
    got = lax.all_to_all(
        sent.reshape(PEERS, 1, RECORD_ROWS * TILE), "rows", split_axis=0, concat_axis=0, tiled=True
    )
    got = got.reshape(PEERS * RECORD_ROWS, TILE)
    half_scale = 0.25 / math.sqrt(2.0 * BLOCK * FEAT * edges / (TILE_DEV * BPT))
    across = swap(got, 2)
    up = (shift(got, 1), shift(across, 1))
    down = (shift(got, -1), shift(across, -1))
    own = gather_blocks(half_scale, 0, (got, across, swap(got, 1), swap(across, 1)), w_third)
    (up, down), own = lax.optimization_barrier(((up, down), own))
    before, after = [
        gather_blocks(half_scale, side, (a, b, swap(a, 1), swap(b, 1)), w_third)
        for side, (a, b) in ((-1, up), (1, down))
    ]
    group = lax.axis_index("feat").astype(jnp.int32).reshape(1)
    return purify(group, before, own, after)


def solution(mesh):
    in_specs = (
        P(("rows", "feat"), None),
        P(("rows", "feat"), None),
        P(("rows", "feat")),
        P(("rows", "feat")),
        P(("rows", "feat")),
        P(),
        P(),
        P(),
    )
    out_specs = P("rows", None, "feat", None)
    return jax.shard_map(local, mesh=mesh, in_specs=in_specs, out_specs=out_specs, check_vma=False)
```

```python
import functools
import math

import jax
import jax.numpy as jnp
from jax import lax
from jax.experimental import pallas as pl
from jax.experimental.pallas import tpu as pltpu
from jax.sharding import PartitionSpec as P

BLOCK = 16
TILE = 128
BAND = 9
HALF = BAND // 2
TILE_DEV = 8
BPT = TILE // BLOCK
F = 256
CAP = 4
PEERS = 128
FIRST_ROWS = CAP + 1
REST_ROWS = CAP
FEAT = 4
COLS = TILE // FEAT
BF = jnp.bfloat16
F32 = jnp.float32


def dot(a, b):
    return jnp.dot(a, b, preferred_element_type=F32)


def dot_t(a, b):
    return lax.dot_general(a, b, (((1,), (1,)), ((), ())), preferred_element_type=F32)


def pieces(x):
    high = x.astype(BF)
    return high, (x - high.astype(F32)).astype(BF)


def slot_rows(k, first, rest):
    if k < CAP // 2:
        return first, 2 * k, FIRST_ROWS
    return rest, 2 * k - CAP, REST_ROWS


def pack_kernel(feats, owner, src, slot, dst, w_first, w_second, out_first, out_rest):
    edges = feats.shape[0]
    hidden = jax.nn.silu(dot(feats[...], w_first[...])).astype(BF)
    hidden = jax.nn.silu(dot(hidden, w_second[...])).astype(BF)
    named = lax.broadcasted_iota(jnp.int32, (PEERS, edges), 0) == owner[...]
    onehot = named.astype(F32)
    before = lax.broadcasted_iota(jnp.int32, (edges, edges), 0) < lax.broadcasted_iota(
        jnp.int32, (edges, edges), 1
    )
    earlier = dot(onehot.astype(BF), before.astype(F32).astype(BF))
    rank = jnp.sum(onehot * earlier, axis=0, keepdims=True)
    src_v, slot_v, dst_v = src[...], slot[...], dst[...]
    tile_code = ((src_v // BPT) * BAND + slot_v).astype(F32)
    block_code = ((src_v % BPT) * BPT + dst_v).astype(F32)
    lane = lax.broadcasted_iota(jnp.int32, (PEERS, TILE), 1)
    codes = jnp.zeros((PEERS, TILE), F32)
    for k in range(CAP):
        chosen = jnp.where(rank == float(k), onehot, 0.0)
        placed = dot(chosen.astype(BF), hidden)
        out, row, stride = slot_rows(k, out_first, out_rest)
        out[pl.ds(row, PEERS, stride=stride), :] = placed[:, :TILE]
        out[pl.ds(row + 1, PEERS, stride=stride), :] = placed[:, TILE:]
        tile_of = jnp.sum(chosen * tile_code, axis=1, keepdims=True)
        block_of = jnp.sum(chosen * block_code, axis=1, keepdims=True)
        codes = codes + jnp.where(lane == k, tile_of, 0.0)
        codes = codes + jnp.where(lane == CAP + k, block_of, 0.0)
    out_first[pl.ds(CAP, PEERS, stride=FIRST_ROWS), :] = codes


def pack(feats, owner, src, slot, dst, w_first, w_second):
    return pl.pallas_call(
        pack_kernel,
        out_shape=[
            jax.ShapeDtypeStruct((PEERS * FIRST_ROWS, TILE), F32),
            jax.ShapeDtypeStruct((PEERS * REST_ROWS, TILE), F32),
        ],
        name="pack",
    )(feats, owner, src, slot, dst, w_first, w_second)


RECORDS = FEAT * CAP * PEERS
OUTER = 4 * BAND + 10


def kept_tile(side, i, s):
    if side == 0:
        return i * BAND + s
    if side < 0:
        inner, outer = i - 4, 36 + i * (i + 1) // 2 + s - (8 - i)
        return jnp.where(i >= 4, inner * BAND + s, jnp.where(s >= 8 - i, outer, -1))
    m = i - 4
    outer = 36 + m * (9 - m) // 2 + s
    return jnp.where(i < 4, i * BAND + s, jnp.where(s <= 3 - m, outer, -1))


def gather_kernel(scale, side, a0, a1, b0, b1, w_third, out, hid, code, spread):
    tiles = out.shape[0]
    rows_t = tiles * BPT
    for f in range(FEAT):
        first = (a0, a1)[f // 2].at[pl.ds(f % 2 * PEERS * FIRST_ROWS, PEERS * FIRST_ROWS), :]
        rest = (b0, b1)[f // 2].at[pl.ds(f % 2 * PEERS * REST_ROWS, PEERS * REST_ROWS), :]
        codes = jnp.transpose(first[pl.ds(CAP, PEERS, stride=FIRST_ROWS), :]).astype(jnp.int32)
        for k in range(CAP):
            at = (f * CAP + k) * PEERS
            blk, row, stride = slot_rows(k, first, rest)
            for half in range(2):
                hid[at : at + PEERS, half * TILE : (half + 1) * TILE] = blk[
                    pl.ds(row + half, PEERS, stride=stride), :
                ].astype(BF)
            tile_of, block_of = codes[k : k + 1, :], codes[CAP + k : CAP + k + 1, :]
            tile_of = kept_tile(side, tile_of // BAND, tile_of % BAND)
            place_of = (block_of % BPT) * rows_t + tile_of * BPT + block_of // BPT
            code[0:1, at : at + PEERS] = jnp.where(tile_of >= 0, place_of, -1)
    w = w_third[...].astype(F32)
    w = [
        jnp.concatenate(
            [w[:, g * 64 + h * COLS : g * 64 + (h + 1) * COLS] for g in range(FEAT)], axis=1
        )
        for h in range(2)
    ]

    def place(b, carry):
        turned = [pltpu.roll(x, 4 * b, 1).astype(BF) for x in w]
        spot = lax.broadcasted_iota(jnp.int32, (rows_t, RECORDS), 0) + b * rows_t
        onehot = jnp.where(spot == code[0:1, :], 1.0, 0.0).astype(BF)
        high, low = pieces(dot(onehot, hid[...]))
        turned = jnp.concatenate(turned, axis=1)
        spread[b] = (dot(high, turned) + dot(low, turned)) * scale
        return carry

    lax.fori_loop(0, BPT, place, 0)
    turn = (lax.broadcasted_iota(jnp.int32, (BPT, TILE), 1) // 4) % BPT

    def arrange(step, carry):
        for t in (2 * step, 2 * step + 1):
            rows = pl.ds(pl.multiple_of(t * BPT, BPT), BPT)
            for half in range(2):
                x = [
                    spread[(BPT - j) % BPT, rows, half * TILE : (half + 1) * TILE]
                    for j in range(BPT)
                ]
                for bit in (1, 2, 4):
                    moved = (turn // bit) % 2 == 1
                    x = [jnp.where(moved, x[(j - bit) % BPT], x[j]) for j in range(BPT)]
                for q in range(BPT):
                    comp = half * BPT + q
                    first = (comp // 4) * COLS + comp % 4
                    y = pltpu.roll(x[q], TILE - 4 * q, 1) if q else x[q]
                    out[t, pl.ds(first, BPT, stride=4), :] = y
        return carry

    lax.fori_loop(0, tiles // 2, arrange, 0)


def gather_blocks(scale, side, blocks, w):
    tiles = OUTER if side else TILE_DEV * BAND
    rows_t = tiles * BPT
    return pl.pallas_call(
        functools.partial(gather_kernel, scale, side),
        out_shape=jax.ShapeDtypeStruct((tiles, TILE, TILE), F32),
        scratch_shapes=[
            pltpu.VMEM((RECORDS, F), BF),
            pltpu.VMEM((8, RECORDS), jnp.int32),
            pltpu.VMEM((BPT, rows_t, F), F32),
        ],
        compiler_params=pltpu.CompilerParams(vmem_limit_bytes=56 * 2**20),
        cost_estimate=pl.CostEstimate(
            flops=2 * BPT * rows_t * F * (RECORDS + 2 * F),
            bytes_accessed=7 * 2**20,
            transcendentals=0,
        ),
        name="gather_blocks",
    )(*blocks, w)


PAIR = 2 * TILE
SPAN = 5 * PAIR
INNER = 8
SLICE = 2 * COLS


def purify_kernel(group, before, own, after, out, e_hi, e_lo, f_hi, f_lo, g_hi, g_lo, s_hi, s_lo):
    def tile(a, s):
        if a < 4:
            return before[36 + a * (a + 1) // 2 + s - (8 - a)]
        if a < 8:
            return before[(a - 4) * BAND + s]
        if a < 16:
            return own[(a - 8) * BAND + s]
        if a < 20:
            return after[(a - 16) * BAND + s]
        return after[36 + (a - 20) * (29 - a) // 2 + s]

    zero = jnp.zeros((TILE, TILE), BF)
    for p in range(INNER):
        for par in range(2):
            a = 2 * (p + 2) + par
            rows = slice(par * TILE, (par + 1) * TILE)
            edge = slice(0, TILE) if par else slice(9 * TILE, 10 * TILE)
            e_hi[p, rows, edge] = zero
            e_lo[p, rows, edge] = zero
            for s in range(BAND):
                x = tile(a, s) + jnp.transpose(tile(a + s - HALF, BAND - 1 - s))
                at = slice((s + par) * TILE, (s + par + 1) * TILE)
                e_hi[p, rows, at], e_lo[p, rows, at] = pieces(x)

    mine = pl.multiple_of(group[0] * COLS, COLS)
    row_tile = lax.broadcasted_iota(jnp.int32, (PAIR, PAIR), 0) // TILE
    col_tile = lax.broadcasted_iota(jnp.int32, (PAIR, PAIR), 1) // TILE

    def product(a_hi, a_lo, b_hi, b_lo):
        return dot_t(a_hi, b_hi) + (dot_t(a_hi, b_lo) + dot_t(a_lo, b_hi))

    def square(d, p, carry):
        o = p + d
        k = SPAN - d * PAIR
        at = slice((2 + d) * PAIR, (3 + d) * PAIR)
        x = product(e_hi[p, :, d * PAIR :], e_lo[p, :, d * PAIR :], e_hi[o, :, :k], e_lo[o, :, :k])
        if d == 2:
            x = jnp.where(col_tile > row_tile, 0.0, x)
        x = x + (e_hi[p, :, at].astype(F32) + e_lo[p, :, at].astype(F32))
        f_hi[p, :, at], f_lo[p, :, at] = pieces(x)
        if d:
            back = slice((2 - d) * PAIR, (3 - d) * PAIR)
            f_hi[o, :, back], f_lo[o, :, back] = pieces(jnp.transpose(x))
        return carry

    for d, first in ((0, 2), (1, 1), (2, 0)):
        lax.fori_loop(first, 6, functools.partial(square, d), 0)

    g_hi[...] = jnp.zeros_like(g_hi)
    g_lo[...] = jnp.zeros_like(g_lo)
    for p in range(INNER):
        rows = slice(p * SLICE, (p + 1) * SLICE)
        outside = (0, 1) if p < 2 else (6, 7) if p > 5 else ()
        others = [o for o in range(max(0, p - 2), min(INNER, p + 3)) if o not in outside]
        low, high = others[0], others[-1] + 1
        source = slice((low - p + 2) * PAIR, (high - p + 2) * PAIR)
        for par in range(2):
            from_rows = pl.ds(par * TILE + mine, COLS)
            to_rows = slice(p * SLICE + par * COLS, p * SLICE + (par + 1) * COLS)
            for g_ref, f_ref in ((g_hi, f_hi), (g_lo, f_lo)):
                g_ref[to_rows, low * PAIR : high * PAIR] = f_ref[p, from_rows, source]
            if outside:
                for s_ref, e_ref in ((s_hi, e_hi), (s_lo, e_lo)):
                    s_ref[par * COLS : (par + 1) * COLS, :] = e_ref[p, from_rows, :]
        for o in outside:
            left, right = max(0, o - p) * PAIR, max(0, p - o) * PAIR
            k = SPAN - abs(o - p) * PAIR
            x = product(
                s_hi[:, left : left + k], s_lo[:, left : left + k],
                e_hi[o, :, right : right + k], e_lo[o, :, right : right + k],
            )
            at = slice((o - p + 2) * PAIR, (o - p + 3) * PAIR)
            x = x + (s_hi[:, at].astype(F32) + s_lo[:, at].astype(F32))
            g_hi[rows, o * PAIR : (o + 1) * PAIR], g_lo[rows, o * PAIR : (o + 1) * PAIR] = pieces(x)

    diagonal = lax.broadcasted_iota(jnp.int32, (COLS, TILE), 0) + mine == (
        lax.broadcasted_iota(jnp.int32, (COLS, TILE), 1)
    )
    diagonal = jnp.where(diagonal, 7.0 / 16.0, 0.0)
    for m in range(4):
        p = m + 2
        rows = slice(m * SLICE, (m + 5) * SLICE)
        span = slice(m * PAIR, (m + 5) * PAIR)
        at = slice(p * PAIR, (p + 1) * PAIR)
        x = product(g_hi[rows, span], g_lo[rows, span], f_hi[p], f_lo[p])
        x = 1.5 * (g_hi[rows, at].astype(F32) + g_lo[rows, at].astype(F32)) - x
        for par in range(2):
            for s in range(BAND):
                y = x[(s + par) * COLS : (s + par + 1) * COLS, par * TILE : (par + 1) * TILE]
                if s == HALF:
                    y = y + diagonal
                out[2 * m + par, s] = y


def purify(group, before, own, after):
    return pl.pallas_call(
        purify_kernel,
        out_shape=jax.ShapeDtypeStruct((TILE_DEV, BAND, COLS, TILE), F32),
        in_specs=[pl.BlockSpec(memory_space=pltpu.SMEM)]
        + [pl.BlockSpec(memory_space=pltpu.VMEM)] * 3,
        scratch_shapes=[pltpu.VMEM((INNER, PAIR, SPAN), BF)] * 4
        + [pltpu.VMEM((INNER * SLICE, INNER * PAIR), BF)] * 2
        + [pltpu.VMEM((SLICE, SPAN), BF)] * 2,
        compiler_params=pltpu.CompilerParams(vmem_limit_bytes=60 * 2**20),
        name="purify",
    )(group, before, own, after)


def exchange(x):
    x = x.reshape(PEERS, 1, -1)
    return lax.all_to_all(x, "rows", split_axis=0, concat_axis=0, tiled=True).reshape(-1, TILE)


def swap(x, axis_bit):
    pairs = [(r * FEAT + g, r * FEAT + (g ^ axis_bit)) for r in range(PEERS) for g in range(FEAT)]
    return lax.ppermute(x, ("rows", "feat"), pairs)


def shift(x, step):
    pairs = [(r, (r + step) % PEERS) for r in range(PEERS)]
    return lax.ppermute(x, "rows", pairs)


def local(edge_feats, edge_owner, src_local, band_slot, dst_local, w_first, w_second, w_third):
    edges = edge_feats.shape[0]
    row = lambda x: x.reshape(1, edges)
    first, rest = pack(
        edge_feats, row(edge_owner), row(src_local), row(band_slot), row(dst_local),
        w_first, w_second,
    )
    half_scale = 0.25 / math.sqrt(2.0 * BLOCK * FEAT * edges / (TILE_DEV * BPT))
    first = exchange(first)
    first, rest = lax.optimization_barrier((first, rest))
    rest = exchange(rest)
    first = jnp.concatenate([first, swap(first, 2)], axis=0)
    first_up, first_down = shift(first, 1), shift(first, -1)
    first, first_up, first_down, rest = lax.optimization_barrier(
        (first, first_up, first_down, rest)
    )
    rest = jnp.concatenate([rest, swap(rest, 2)], axis=0)
    rest_up = shift(rest, 1)
    own = gather_blocks(
        half_scale, 0, (first, swap(first, 1), rest, swap(rest, 1)), w_third
    )
    rest, rest_up, own = lax.optimization_barrier((rest, rest_up, own))
    rest_down = shift(rest, -1)
    before = gather_blocks(
        half_scale, -1, (first_up, swap(first_up, 1), rest_up, swap(rest_up, 1)), w_third
    )
    rest_down, before = lax.optimization_barrier((rest_down, before))
    after = gather_blocks(
        half_scale, 1, (first_down, swap(first_down, 1), rest_down, swap(rest_down, 1)), w_third
    )
    group = lax.axis_index("feat").astype(jnp.int32).reshape(1)
    return purify(group, before, own, after)


def solution(mesh):
    in_specs = (
        P(("rows", "feat"), None),
        P(("rows", "feat"), None),
        P(("rows", "feat")),
        P(("rows", "feat")),
        P(("rows", "feat")),
        P(),
        P(),
        P(),
    )
    out_specs = P("rows", None, "feat", None)
    return jax.shard_map(local, mesh=mesh, in_specs=in_specs, out_specs=out_specs, check_vma=False)
```

```python
import functools
import math

import jax
import jax.numpy as jnp
from jax import lax
from jax.experimental import pallas as pl
from jax.experimental.pallas import tpu as pltpu
from jax.sharding import PartitionSpec as P

BLOCK = 16
TILE = 128
BAND = 9
HALF = BAND // 2
TILE_DEV = 8
BPT = TILE // BLOCK
F = 256
CAP = 4
PEERS = 128
RECORD_ROWS = 2 * CAP + 1
FEAT = 4
COLS = TILE // FEAT
BF = jnp.bfloat16
F32 = jnp.float32


def dot(a, b):
    return jnp.dot(a, b, preferred_element_type=F32)


def dot_t(a, b):
    return lax.dot_general(a, b, (((1,), (1,)), ((), ())), preferred_element_type=F32)


def pieces(x):
    high = x.astype(BF)
    return high, (x - high.astype(F32)).astype(BF)


def pack_kernel(feats, owner, src, slot, dst, w_first, w_second, out):
    edges = feats.shape[0]
    hidden = jax.nn.silu(dot(feats[...], w_first[...])).astype(BF)
    hidden = jax.nn.silu(dot(hidden, w_second[...])).astype(BF)
    named = lax.broadcasted_iota(jnp.int32, (PEERS, edges), 0) == owner[...]
    onehot = named.astype(F32)
    before = lax.broadcasted_iota(jnp.int32, (edges, edges), 0) < lax.broadcasted_iota(
        jnp.int32, (edges, edges), 1
    )
    earlier = dot(onehot.astype(BF), before.astype(F32).astype(BF))
    rank = jnp.sum(onehot * earlier, axis=0, keepdims=True)
    src_v, slot_v, dst_v = src[...], slot[...], dst[...]
    tile_code = ((src_v // BPT) * BAND + slot_v).astype(F32)
    block_code = ((src_v % BPT) * BPT + dst_v).astype(F32)
    lane = lax.broadcasted_iota(jnp.int32, (PEERS, TILE), 1)
    codes = jnp.zeros((PEERS, TILE), F32)
    for k in range(CAP):
        chosen = jnp.where(rank == float(k), onehot, 0.0)
        placed = dot(chosen.astype(BF), hidden)
        out[pl.ds(2 * k, PEERS, stride=RECORD_ROWS), :] = placed[:, :TILE]
        out[pl.ds(2 * k + 1, PEERS, stride=RECORD_ROWS), :] = placed[:, TILE:]
        tile_of = jnp.sum(chosen * tile_code, axis=1, keepdims=True)
        block_of = jnp.sum(chosen * block_code, axis=1, keepdims=True)
        codes = codes + jnp.where(lane == k, tile_of, 0.0)
        codes = codes + jnp.where(lane == CAP + k, block_of, 0.0)
    out[pl.ds(2 * CAP, PEERS, stride=RECORD_ROWS), :] = codes


def pack(feats, owner, src, slot, dst, w_first, w_second):
    return pl.pallas_call(
        pack_kernel,
        out_shape=jax.ShapeDtypeStruct((PEERS * RECORD_ROWS, TILE), F32),
        name="pack",
    )(feats, owner, src, slot, dst, w_first, w_second)


RECORDS = FEAT * CAP * PEERS
OUTER = 4 * BAND + 10


def kept_tile(side, i, s):
    if side == 0:
        return i * BAND + s
    if side < 0:
        inner, outer = i - 4, 36 + i * (i + 1) // 2 + s - (8 - i)
        return jnp.where(i >= 4, inner * BAND + s, jnp.where(s >= 8 - i, outer, -1))
    m = i - 4
    outer = 36 + m * (9 - m) // 2 + s
    return jnp.where(i < 4, i * BAND + s, jnp.where(s <= 3 - m, outer, -1))


def gather_kernel(scale, side, b0, b1, w_third, out, hid, code, spread):
    tiles = out.shape[0]
    rows_t = tiles * BPT
    for f in range(FEAT):
        blk = (b0, b1)[f // 2].at[pl.ds(f % 2 * PEERS * RECORD_ROWS, PEERS * RECORD_ROWS), :]
        codes = jnp.transpose(blk[pl.ds(2 * CAP, PEERS, stride=RECORD_ROWS), :]).astype(jnp.int32)
        for k in range(CAP):
            at = (f * CAP + k) * PEERS
            for half in range(2):
                hid[at : at + PEERS, half * TILE : (half + 1) * TILE] = blk[
                    pl.ds(2 * k + half, PEERS, stride=RECORD_ROWS), :
                ].astype(BF)
            tile_of, block_of = codes[k : k + 1, :], codes[CAP + k : CAP + k + 1, :]
            tile_of = kept_tile(side, tile_of // BAND, tile_of % BAND)
            place_of = (block_of % BPT) * rows_t + tile_of * BPT + block_of // BPT
            code[0:1, at : at + PEERS] = jnp.where(tile_of >= 0, place_of, -1)
    w = w_third[...].astype(F32)
    w = [
        jnp.concatenate(
            [w[:, g * 64 + h * COLS : g * 64 + (h + 1) * COLS] for g in range(FEAT)], axis=1
        )
        for h in range(2)
    ]

    def place(b, carry):
        turned = [pltpu.roll(x, 4 * b, 1).astype(BF) for x in w]
        spot = lax.broadcasted_iota(jnp.int32, (rows_t, RECORDS), 0) + b * rows_t
        onehot = jnp.where(spot == code[0:1, :], 1.0, 0.0).astype(BF)
        high, low = pieces(dot(onehot, hid[...]))
        turned = jnp.concatenate(turned, axis=1)
        spread[b] = (dot(high, turned) + dot(low, turned)) * scale
        return carry

    lax.fori_loop(0, BPT, place, 0)
    turn = (lax.broadcasted_iota(jnp.int32, (BPT, TILE), 1) // 4) % BPT

    def arrange(step, carry):
        for t in (2 * step, 2 * step + 1):
            rows = pl.ds(pl.multiple_of(t * BPT, BPT), BPT)
            for half in range(2):
                x = [
                    spread[(BPT - j) % BPT, rows, half * TILE : (half + 1) * TILE]
                    for j in range(BPT)
                ]
                for bit in (1, 2, 4):
                    moved = (turn // bit) % 2 == 1
                    x = [jnp.where(moved, x[(j - bit) % BPT], x[j]) for j in range(BPT)]
                for q in range(BPT):
                    comp = half * BPT + q
                    first = (comp // 4) * COLS + comp % 4
                    y = pltpu.roll(x[q], TILE - 4 * q, 1) if q else x[q]
                    out[t, pl.ds(first, BPT, stride=4), :] = y
        return carry

    lax.fori_loop(0, tiles // 2, arrange, 0)


def gather_blocks(scale, side, blocks, w):
    tiles = OUTER if side else TILE_DEV * BAND
    rows_t = tiles * BPT
    return pl.pallas_call(
        functools.partial(gather_kernel, scale, side),
        out_shape=jax.ShapeDtypeStruct((tiles, TILE, TILE), F32),
        scratch_shapes=[
            pltpu.VMEM((RECORDS, F), BF),
            pltpu.VMEM((8, RECORDS), jnp.int32),
            pltpu.VMEM((BPT, rows_t, F), F32),
        ],
        compiler_params=pltpu.CompilerParams(vmem_limit_bytes=56 * 2**20),
        cost_estimate=pl.CostEstimate(
            flops=2 * BPT * rows_t * F * (RECORDS + 2 * F),
            bytes_accessed=7 * 2**20,
            transcendentals=0,
        ),
        name="gather_blocks",
    )(*blocks, w)


PAIR = 2 * TILE
SPAN = 5 * PAIR
INNER = 8
SLICE = 2 * COLS


def purify_kernel(group, before, own, after, out, e_hi, e_lo, f_hi, f_lo, g_hi, g_lo, s_hi, s_lo):
    def tile(a, s):
        if a < 4:
            return before[36 + a * (a + 1) // 2 + s - (8 - a)]
        if a < 8:
            return before[(a - 4) * BAND + s]
        if a < 16:
            return own[(a - 8) * BAND + s]
        if a < 20:
            return after[(a - 16) * BAND + s]
        return after[36 + (a - 20) * (29 - a) // 2 + s]

    zero = jnp.zeros((TILE, TILE), BF)
    for p in range(INNER):
        for par in range(2):
            a = 2 * (p + 2) + par
            rows = slice(par * TILE, (par + 1) * TILE)
            edge = slice(0, TILE) if par else slice(9 * TILE, 10 * TILE)
            e_hi[p, rows, edge] = zero
            e_lo[p, rows, edge] = zero
            for s in range(BAND):
                x = tile(a, s) + jnp.transpose(tile(a + s - HALF, BAND - 1 - s))
                at = slice((s + par) * TILE, (s + par + 1) * TILE)
                e_hi[p, rows, at], e_lo[p, rows, at] = pieces(x)

    mine = pl.multiple_of(group[0] * COLS, COLS)
    row_tile = lax.broadcasted_iota(jnp.int32, (PAIR, PAIR), 0) // TILE
    col_tile = lax.broadcasted_iota(jnp.int32, (PAIR, PAIR), 1) // TILE

    def product(a_hi, a_lo, b_hi, b_lo):
        rows = a_hi.shape[0]
        both = dot_t(jnp.concatenate([a_hi, a_lo], axis=0), b_hi)
        return both[:rows] + (both[rows:] + dot_t(a_hi, b_lo))

    def square(d, p, carry):
        o = p + d
        k = SPAN - d * PAIR
        at = slice((2 + d) * PAIR, (3 + d) * PAIR)
        x = product(e_hi[p, :, d * PAIR :], e_lo[p, :, d * PAIR :], e_hi[o, :, :k], e_lo[o, :, :k])
        if d == 2:
            x = jnp.where(col_tile > row_tile, 0.0, x)
        x = x + (e_hi[p, :, at].astype(F32) + e_lo[p, :, at].astype(F32))
        f_hi[p, :, at], f_lo[p, :, at] = pieces(x)
        if d:
            back = slice((2 - d) * PAIR, (3 - d) * PAIR)
            f_hi[o, :, back], f_lo[o, :, back] = pieces(jnp.transpose(x))
        return carry

    for d, first in ((0, 2), (1, 1), (2, 0)):
        lax.fori_loop(first, 6, functools.partial(square, d), 0)

    g_hi[...] = jnp.zeros_like(g_hi)
    g_lo[...] = jnp.zeros_like(g_lo)
    for p in range(INNER):
        outside = (0, 1) if p < 2 else (6, 7) if p > 5 else ()
        others = [o for o in range(max(0, p - 2), min(INNER, p + 3)) if o not in outside]
        low, high = others[0], others[-1] + 1
        source = slice((low - p + 2) * PAIR, (high - p + 2) * PAIR)
        for par in range(2):
            from_rows = pl.ds(par * TILE + mine, COLS)
            to_rows = slice(p * SLICE + par * COLS, p * SLICE + (par + 1) * COLS)
            for g_ref, f_ref in ((g_hi, f_hi), (g_lo, f_lo)):
                g_ref[to_rows, low * PAIR : high * PAIR] = f_ref[p, from_rows, source]
    for base in (0, 6):
        s_hi[...] = jnp.zeros_like(s_hi)
        s_lo[...] = jnp.zeros_like(s_lo)
        for i in range(2):
            for par in range(2):
                from_rows = pl.ds(par * TILE + mine, COLS)
                to_rows = slice(i * SLICE + par * COLS, i * SLICE + (par + 1) * COLS)
                for s_ref, e_ref in ((s_hi, e_hi), (s_lo, e_lo)):
                    s_ref[to_rows, i * PAIR : i * PAIR + SPAN] = e_ref[base + i, from_rows, :]
        for i in range(2):
            o = base + i
            span = slice(i * PAIR, i * PAIR + SPAN)
            x = product(s_hi[:, span], s_lo[:, span], e_hi[o], e_lo[o])
            at = slice((i + 2) * PAIR, (i + 3) * PAIR)
            x = x + (s_hi[:, at].astype(F32) + s_lo[:, at].astype(F32))
            rows = slice(base * SLICE, (base + 2) * SLICE)
            g_hi[rows, o * PAIR : (o + 1) * PAIR], g_lo[rows, o * PAIR : (o + 1) * PAIR] = pieces(x)

    diagonal = lax.broadcasted_iota(jnp.int32, (COLS, TILE), 0) + mine == (
        lax.broadcasted_iota(jnp.int32, (COLS, TILE), 1)
    )
    diagonal = jnp.where(diagonal, 7.0 / 16.0, 0.0)
    for m in range(4):
        p = m + 2
        rows = slice(m * SLICE, (m + 5) * SLICE)
        span = slice(m * PAIR, (m + 5) * PAIR)
        at = slice(p * PAIR, (p + 1) * PAIR)
        x = product(g_hi[rows, span], g_lo[rows, span], f_hi[p], f_lo[p])
        x = 1.5 * (g_hi[rows, at].astype(F32) + g_lo[rows, at].astype(F32)) - x
        for par in range(2):
            for s in range(BAND):
                y = x[(s + par) * COLS : (s + par + 1) * COLS, par * TILE : (par + 1) * TILE]
                if s == HALF:
                    y = y + diagonal
                out[2 * m + par, s] = y


def purify(group, before, own, after):
    return pl.pallas_call(
        purify_kernel,
        out_shape=jax.ShapeDtypeStruct((TILE_DEV, BAND, COLS, TILE), F32),
        in_specs=[pl.BlockSpec(memory_space=pltpu.SMEM)]
        + [pl.BlockSpec(memory_space=pltpu.VMEM)] * 3,
        scratch_shapes=[pltpu.VMEM((INNER, PAIR, SPAN), BF)] * 4
        + [pltpu.VMEM((INNER * SLICE, INNER * PAIR), BF)] * 2
        + [pltpu.VMEM((2 * SLICE, SPAN + PAIR), BF)] * 2,
        compiler_params=pltpu.CompilerParams(vmem_limit_bytes=60 * 2**20),
        name="purify",
    )(group, before, own, after)


def swap(x, axis_bit):
    pairs = [(r * FEAT + g, r * FEAT + (g ^ axis_bit)) for r in range(PEERS) for g in range(FEAT)]
    return lax.ppermute(x, ("rows", "feat"), pairs)


def shift(x, step):
    count = PEERS * FEAT
    pairs = [(d, (d + step * FEAT) % count) for d in range(count)]
    return lax.ppermute(x, ("rows", "feat"), pairs)


def local(edge_feats, edge_owner, src_local, band_slot, dst_local, w_first, w_second, w_third):
    edges = edge_feats.shape[0]
    row = lambda x: x.reshape(1, edges)
    sent = pack(
        edge_feats, row(edge_owner), row(src_local), row(band_slot), row(dst_local),
        w_first, w_second,
    )
    got = lax.all_to_all(
        sent.reshape(PEERS, 1, RECORD_ROWS * TILE), "rows", split_axis=0, concat_axis=0, tiled=True
    )
    got = got.reshape(PEERS * RECORD_ROWS, TILE)
    half_scale = 0.25 / math.sqrt(2.0 * BLOCK * FEAT * edges / (TILE_DEV * BPT))
    held = jnp.concatenate([got, swap(got, 2)], axis=0)
    up = shift(held, 1)
    own = gather_blocks(half_scale, 0, (held, swap(held, 1)), w_third)
    held, up, own = lax.optimization_barrier((held, up, own))
    down = shift(held, -1)
    before = gather_blocks(half_scale, -1, (up, swap(up, 1)), w_third)
    down, before = lax.optimization_barrier((down, before))
    after = gather_blocks(half_scale, 1, (down, swap(down, 1)), w_third)
    group = lax.axis_index("feat").astype(jnp.int32).reshape(1)
    return purify(group, before, own, after)


def solution(mesh):
    in_specs = (
        P(("rows", "feat"), None),
        P(("rows", "feat"), None),
        P(("rows", "feat")),
        P(("rows", "feat")),
        P(("rows", "feat")),
        P(),
        P(),
        P(),
    )
    out_specs = P("rows", None, "feat", None)
    return jax.shard_map(local, mesh=mesh, in_specs=in_specs, out_specs=out_specs, check_vma=False)
```

```python
import functools
import math

import jax
import jax.numpy as jnp
from jax import lax
from jax.experimental import pallas as pl
from jax.experimental.pallas import tpu as pltpu
from jax.sharding import PartitionSpec as P

BLOCK = 16
TILE = 128
BAND = 9
HALF = BAND // 2
TILE_DEV = 8
BPT = TILE // BLOCK
F = 256
CAP = 4
PEERS = 128
RECORD_ROWS = 2 * CAP + 1
FEAT = 4
COLS = TILE // FEAT
BF = jnp.bfloat16
F32 = jnp.float32


def dot(a, b):
    return jnp.dot(a, b, preferred_element_type=F32)


def dot_t(a, b):
    return lax.dot_general(a, b, (((1,), (1,)), ((), ())), preferred_element_type=F32)


def pieces(x):
    high = x.astype(BF)
    return high, (x - high.astype(F32)).astype(BF)


def pack_kernel(feats, owner, src, slot, dst, w_first, w_second, out):
    edges = feats.shape[0]
    hidden = jax.nn.silu(dot(feats[...], w_first[...])).astype(BF)
    hidden = jax.nn.silu(dot(hidden, w_second[...])).astype(BF)
    named = lax.broadcasted_iota(jnp.int32, (PEERS, edges), 0) == owner[...]
    onehot = named.astype(F32)
    before = lax.broadcasted_iota(jnp.int32, (edges, edges), 0) < lax.broadcasted_iota(
        jnp.int32, (edges, edges), 1
    )
    earlier = dot(onehot.astype(BF), before.astype(F32).astype(BF))
    rank = jnp.sum(onehot * earlier, axis=0, keepdims=True)
    src_v, slot_v, dst_v = src[...], slot[...], dst[...]
    tile_code = ((src_v // BPT) * BAND + slot_v).astype(F32)
    block_code = ((src_v % BPT) * BPT + dst_v).astype(F32)
    lane = lax.broadcasted_iota(jnp.int32, (PEERS, TILE), 1)
    codes = jnp.zeros((PEERS, TILE), F32)
    for k in range(CAP):
        chosen = jnp.where(rank == float(k), onehot, 0.0)
        placed = dot(chosen.astype(BF), hidden)
        out[pl.ds(2 * k, PEERS, stride=RECORD_ROWS), :] = placed[:, :TILE]
        out[pl.ds(2 * k + 1, PEERS, stride=RECORD_ROWS), :] = placed[:, TILE:]
        tile_of = jnp.sum(chosen * tile_code, axis=1, keepdims=True)
        block_of = jnp.sum(chosen * block_code, axis=1, keepdims=True)
        codes = codes + jnp.where(lane == k, tile_of, 0.0)
        codes = codes + jnp.where(lane == CAP + k, block_of, 0.0)
    out[pl.ds(2 * CAP, PEERS, stride=RECORD_ROWS), :] = codes


def pack(feats, owner, src, slot, dst, w_first, w_second):
    return pl.pallas_call(
        pack_kernel,
        out_shape=jax.ShapeDtypeStruct((PEERS * RECORD_ROWS, TILE), F32),
        name="pack",
    )(feats, owner, src, slot, dst, w_first, w_second)


RECORDS = FEAT * CAP * PEERS
OUTER = 4 * BAND + 10


def kept_tile(i, s, earlier):
    inner, outer = i - 4, 36 + i * (i + 1) // 2 + s - (8 - i)
    before = jnp.where(i >= 4, inner * BAND + s, jnp.where(s >= 8 - i, outer, -1))
    m = i - 4
    outer = 36 + m * (9 - m) // 2 + s
    after = jnp.where(i < 4, i * BAND + s, jnp.where(s <= 3 - m, outer, -1))
    return jnp.where(earlier, before, after)


def gather_kernel(scale, core, b0, b1, w_third, out, hid, code, spread):
    tiles = out.shape[0]
    rows_t = tiles * BPT
    for f in range(FEAT):
        blk = (b0, b1)[f // 2].at[pl.ds(f % 2 * PEERS * RECORD_ROWS, PEERS * RECORD_ROWS), :]
        codes = jnp.transpose(blk[pl.ds(2 * CAP, PEERS, stride=RECORD_ROWS), :]).astype(jnp.int32)
        for k in range(CAP):
            at = (f * CAP + k) * PEERS
            for half in range(2):
                hid[at : at + PEERS, half * TILE : (half + 1) * TILE] = blk[
                    pl.ds(2 * k + half, PEERS, stride=RECORD_ROWS), :
                ].astype(BF)
            tile_of, block_of = codes[k : k + 1, :], codes[CAP + k : CAP + k + 1, :]
            if tiles == OUTER:
                tile_of = kept_tile(tile_of // BAND, tile_of % BAND, core[0] == 0)
            place_of = (block_of % BPT) * rows_t + tile_of * BPT + block_of // BPT
            code[0:1, at : at + PEERS] = jnp.where(tile_of >= 0, place_of, -1)
    w = w_third[...].astype(F32)
    w = [
        jnp.concatenate(
            [w[:, g * 64 + h * COLS : g * 64 + (h + 1) * COLS] for g in range(FEAT)], axis=1
        )
        for h in range(2)
    ]

    def place(b, carry):
        turned = [pltpu.roll(x, 4 * b, 1).astype(BF) for x in w]
        spot = lax.broadcasted_iota(jnp.int32, (rows_t, RECORDS), 0) + b * rows_t
        onehot = jnp.where(spot == code[0:1, :], 1.0, 0.0).astype(BF)
        high, low = pieces(dot(onehot, hid[...]))
        turned = jnp.concatenate(turned, axis=1)
        spread[b] = (dot(high, turned) + dot(low, turned)) * scale
        return carry

    lax.fori_loop(0, BPT, place, 0)
    turn = (lax.broadcasted_iota(jnp.int32, (BPT, TILE), 1) // 4) % BPT

    def arrange(step, carry):
        for t in (2 * step, 2 * step + 1):
            rows = pl.ds(pl.multiple_of(t * BPT, BPT), BPT)
            for half in range(2):
                x = [
                    spread[(BPT - j) % BPT, rows, half * TILE : (half + 1) * TILE]
                    for j in range(BPT)
                ]
                for bit in (1, 2, 4):
                    moved = (turn // bit) % 2 == 1
                    x = [jnp.where(moved, x[(j - bit) % BPT], x[j]) for j in range(BPT)]
                for q in range(BPT):
                    comp = half * BPT + q
                    first = (comp // 4) * COLS + comp % 4
                    y = pltpu.roll(x[q], TILE - 4 * q, 1) if q else x[q]
                    out[t, pl.ds(first, BPT, stride=4), :] = y
        return carry

    lax.fori_loop(0, tiles // 2, arrange, 0)


def gather_blocks(scale, core, tiles, blocks, w):
    rows_t = tiles * BPT
    return pl.pallas_call(
        functools.partial(gather_kernel, scale),
        in_specs=[pl.BlockSpec(memory_space=pltpu.SMEM)]
        + [pl.BlockSpec(memory_space=pltpu.VMEM)] * 3,
        out_shape=jax.ShapeDtypeStruct((tiles, TILE, TILE), F32),
        scratch_shapes=[
            pltpu.VMEM((RECORDS, F), BF),
            pltpu.VMEM((8, RECORDS), jnp.int32),
            pltpu.VMEM((BPT, rows_t, F), F32),
        ],
        compiler_params=pltpu.CompilerParams(vmem_limit_bytes=56 * 2**20),
        cost_estimate=pl.CostEstimate(
            flops=2 * BPT * rows_t * F * (RECORDS + 2 * F),
            bytes_accessed=7 * 2**20,
            transcendentals=0,
        ),
        name="gather_blocks",
    )(core, *blocks, w)


PAIR = 2 * TILE
SPAN = 5 * PAIR
INNER = 8
SLICE = 2 * COLS


def purify_kernel(
    group, own_in, mine_in, other_in, out, own, sides, e_hi, e_lo, f_hi, f_lo, g_hi, g_lo, s_hi, s_lo, sems
):
    core = group[0] % 2
    copies = [
        pltpu.make_async_copy(own_in, own, sems.at[0]),
        pltpu.make_async_copy(mine_in, sides.at[core], sems.at[1]),
        pltpu.make_async_copy(other_in, sides.at[1 - core], sems.at[2]),
    ]
    for copy in copies:
        copy.start()

    def tile(a, s):
        if a < 4:
            return sides[0, 36 + a * (a + 1) // 2 + s - (8 - a)]
        if a < 8:
            return sides[0, (a - 4) * BAND + s]
        if a < 16:
            return own[(a - 8) * BAND + s]
        if a < 20:
            return sides[1, (a - 16) * BAND + s]
        return sides[1, 36 + (a - 20) * (29 - a) // 2 + s]

    def fill(inside):
        for a in range(4, 20):
            for s in range(BAND):
                b = a + s - HALF
                if inside == (8 <= a < 16 and 8 <= b < 16):
                    p, par = a // 2 - 2, a % 2
                    rows = slice(par * TILE, (par + 1) * TILE)
                    at = slice((s + par) * TILE, (s + par + 1) * TILE)
                    x = tile(a, s) + jnp.transpose(tile(b, BAND - 1 - s))
                    e_hi[p, rows, at], e_lo[p, rows, at] = pieces(x)

    zero = jnp.zeros((TILE, TILE), BF)
    for p in range(INNER):
        for rows, edge in ((slice(0, TILE), slice(9 * TILE, 10 * TILE)), (slice(TILE, PAIR), slice(0, TILE))):
            e_hi[p, rows, edge] = zero
            e_lo[p, rows, edge] = zero
    g_hi[...] = jnp.zeros_like(g_hi)
    g_lo[...] = jnp.zeros_like(g_lo)
    copies[0].wait()
    fill(True)
    copies[1].wait()
    copies[2].wait()
    fill(False)

    mine = pl.multiple_of(group[0] * COLS, COLS)
    row_tile = lax.broadcasted_iota(jnp.int32, (PAIR, PAIR), 0) // TILE
    col_tile = lax.broadcasted_iota(jnp.int32, (PAIR, PAIR), 1) // TILE

    def product(a_hi, a_lo, b_hi, b_lo):
        rows = a_hi.shape[0]
        both = dot_t(jnp.concatenate([a_hi, a_lo], axis=0), b_hi)
        return both[:rows] + (both[rows:] + dot_t(a_hi, b_lo))

    def square(d, p, carry):
        o = p + d
        k = SPAN - d * PAIR
        at = slice((2 + d) * PAIR, (3 + d) * PAIR)
        x = product(e_hi[p, :, d * PAIR :], e_lo[p, :, d * PAIR :], e_hi[o, :, :k], e_lo[o, :, :k])
        if d == 2:
            x = jnp.where(col_tile > row_tile, 0.0, x)
        x = x + (e_hi[p, :, at].astype(F32) + e_lo[p, :, at].astype(F32))
        f_hi[p, :, at], f_lo[p, :, at] = pieces(x)
        if d:
            back = slice((2 - d) * PAIR, (3 - d) * PAIR)
            f_hi[o, :, back], f_lo[o, :, back] = pieces(jnp.transpose(x))
        return carry

    for d, first in ((0, 2), (1, 1), (2, 0)):
        lax.fori_loop(first, 6, functools.partial(square, d), 0)

    for p in range(INNER):
        outside = (0, 1) if p < 2 else (6, 7) if p > 5 else ()
        others = [o for o in range(max(0, p - 2), min(INNER, p + 3)) if o not in outside]
        low, high = others[0], others[-1] + 1
        source = slice((low - p + 2) * PAIR, (high - p + 2) * PAIR)
        for par in range(2):
            from_rows = pl.ds(par * TILE + mine, COLS)
            to_rows = slice(p * SLICE + par * COLS, p * SLICE + (par + 1) * COLS)
            for g_ref, f_ref in ((g_hi, f_hi), (g_lo, f_lo)):
                g_ref[to_rows, low * PAIR : high * PAIR] = f_ref[p, from_rows, source]
    for base in (0, 6):
        s_hi[...] = jnp.zeros_like(s_hi)
        s_lo[...] = jnp.zeros_like(s_lo)
        for i in range(2):
            for par in range(2):
                from_rows = pl.ds(par * TILE + mine, COLS)
                to_rows = slice(i * SLICE + par * COLS, i * SLICE + (par + 1) * COLS)
                for s_ref, e_ref in ((s_hi, e_hi), (s_lo, e_lo)):
                    s_ref[to_rows, i * PAIR : i * PAIR + SPAN] = e_ref[base + i, from_rows, :]
        for i in range(2):
            o = base + i
            span = slice(i * PAIR, i * PAIR + SPAN)
            x = product(s_hi[:, span], s_lo[:, span], e_hi[o], e_lo[o])
            at = slice((i + 2) * PAIR, (i + 3) * PAIR)
            x = x + (s_hi[:, at].astype(F32) + s_lo[:, at].astype(F32))
            rows = slice(base * SLICE, (base + 2) * SLICE)
            g_hi[rows, o * PAIR : (o + 1) * PAIR], g_lo[rows, o * PAIR : (o + 1) * PAIR] = pieces(x)

    diagonal = lax.broadcasted_iota(jnp.int32, (COLS, TILE), 0) + mine == (
        lax.broadcasted_iota(jnp.int32, (COLS, TILE), 1)
    )
    diagonal = jnp.where(diagonal, 7.0 / 16.0, 0.0)
    for m in range(4):
        p = m + 2
        rows = slice(m * SLICE, (m + 5) * SLICE)
        span = slice(m * PAIR, (m + 5) * PAIR)
        at = slice(p * PAIR, (p + 1) * PAIR)
        x = product(g_hi[rows, span], g_lo[rows, span], f_hi[p], f_lo[p])
        x = 1.5 * (g_hi[rows, at].astype(F32) + g_lo[rows, at].astype(F32)) - x
        for par in range(2):
            for s in range(BAND):
                y = x[(s + par) * COLS : (s + par + 1) * COLS, par * TILE : (par + 1) * TILE]
                if s == HALF:
                    y = y + diagonal
                out[2 * m + par, s] = y


def purify(group, own, mine, other):
    return pl.pallas_call(
        purify_kernel,
        out_shape=jax.ShapeDtypeStruct((TILE_DEV, BAND, COLS, TILE), F32),
        in_specs=[pl.BlockSpec(memory_space=pltpu.SMEM)]
        + [pl.BlockSpec(memory_space=pl.ANY)] * 3,
        scratch_shapes=[
            pltpu.VMEM((TILE_DEV * BAND, TILE, TILE), F32),
            pltpu.VMEM((2, OUTER, TILE, TILE), F32),
        ]
        + [pltpu.VMEM((INNER, PAIR, SPAN), BF)] * 4
        + [pltpu.VMEM((INNER * SLICE, INNER * PAIR), BF)] * 2
        + [pltpu.VMEM((2 * SLICE, SPAN + PAIR), BF)] * 2
        + [pltpu.SemaphoreType.DMA((3,))],
        compiler_params=pltpu.CompilerParams(vmem_limit_bytes=60 * 2**20),
        name="purify",
    )(group, own, mine, other)


def swap(x, axis_bit):
    pairs = [(r * FEAT + g, r * FEAT + (g ^ axis_bit)) for r in range(PEERS) for g in range(FEAT)]
    return lax.ppermute(x, ("rows", "feat"), pairs)


def to_neighbour(x, same_core):
    count = PEERS * FEAT
    pairs = []
    for d in range(count):
        core = d % 2 if same_core else 1 - d % 2
        step = FEAT if core == 0 else -FEAT
        pairs.append((d, (d - d % 2 + core + step) % count))
    return lax.ppermute(x, ("rows", "feat"), pairs)


def local(edge_feats, edge_owner, src_local, band_slot, dst_local, w_first, w_second, w_third):
    edges = edge_feats.shape[0]
    row = lambda x: x.reshape(1, edges)
    sent = pack(
        edge_feats, row(edge_owner), row(src_local), row(band_slot), row(dst_local),
        w_first, w_second,
    )
    got = lax.all_to_all(
        sent.reshape(PEERS, 1, RECORD_ROWS * TILE), "rows", split_axis=0, concat_axis=0, tiled=True
    )
    got = got.reshape(PEERS * RECORD_ROWS, TILE)
    half_scale = 0.25 / math.sqrt(2.0 * BLOCK * FEAT * edges / (TILE_DEV * BPT))
    held = jnp.concatenate([got, swap(got, 2)], axis=0)
    near = [to_neighbour(held, True), to_neighbour(held, False)]
    group = lax.axis_index("feat").astype(jnp.int32).reshape(1)
    core = group % 2
    own = gather_blocks(half_scale, core, TILE_DEV * BAND, (held, swap(held, 1)), w_third)
    near, own = lax.optimization_barrier((near, own))
    mine = gather_blocks(half_scale, core, OUTER, near, w_third)
    return purify(group, own, mine, swap(mine, 1))


def solution(mesh):
    in_specs = (
        P(("rows", "feat"), None),
        P(("rows", "feat"), None),
        P(("rows", "feat")),
        P(("rows", "feat")),
        P(("rows", "feat")),
        P(),
        P(),
        P(),
    )
    out_specs = P("rows", None, "feat", None)
    return jax.shard_map(local, mesh=mesh, in_specs=in_specs, out_specs=out_specs, check_vma=False)
```

```python
import functools
import math

import jax
import jax.numpy as jnp
from jax import lax
from jax.experimental import pallas as pl
from jax.experimental.pallas import tpu as pltpu
from jax.sharding import PartitionSpec as P

BLOCK = 16
TILE = 128
BAND = 9
HALF = BAND // 2
TILE_DEV = 8
BPT = TILE // BLOCK
F = 256
CAP = 4
PEERS = 128
RECORD_ROWS = 2 * CAP + 1
FEAT = 4
COLS = TILE // FEAT
BF = jnp.bfloat16
F32 = jnp.float32


def dot(a, b):
    return jnp.dot(a, b, preferred_element_type=F32)


def dot_t(a, b):
    return lax.dot_general(a, b, (((1,), (1,)), ((), ())), preferred_element_type=F32)


def pieces(x):
    high = x.astype(BF)
    return high, (x - high.astype(F32)).astype(BF)


def pack_kernel(feats, owner, src, slot, dst, w_first, w_second, out):
    edges = feats.shape[0]
    hidden = jax.nn.silu(dot(feats[...], w_first[...])).astype(BF)
    hidden = jax.nn.silu(dot(hidden, w_second[...])).astype(BF)
    named = lax.broadcasted_iota(jnp.int32, (PEERS, edges), 0) == owner[...]
    onehot = named.astype(F32)
    before = lax.broadcasted_iota(jnp.int32, (edges, edges), 0) < lax.broadcasted_iota(
        jnp.int32, (edges, edges), 1
    )
    earlier = dot(onehot.astype(BF), before.astype(F32).astype(BF))
    rank = jnp.sum(onehot * earlier, axis=0, keepdims=True)
    src_v, slot_v, dst_v = src[...], slot[...], dst[...]
    tile_code = ((src_v // BPT) * BAND + slot_v).astype(F32)
    block_code = ((src_v % BPT) * BPT + dst_v).astype(F32)
    lane = lax.broadcasted_iota(jnp.int32, (PEERS, TILE), 1)
    codes = jnp.zeros((PEERS, TILE), F32)
    for k in range(CAP):
        chosen = jnp.where(rank == float(k), onehot, 0.0)
        placed = dot(chosen.astype(BF), hidden)
        out[pl.ds(2 * k, PEERS, stride=RECORD_ROWS), :] = placed[:, :TILE]
        out[pl.ds(2 * k + 1, PEERS, stride=RECORD_ROWS), :] = placed[:, TILE:]
        tile_of = jnp.sum(chosen * tile_code, axis=1, keepdims=True)
        block_of = jnp.sum(chosen * block_code, axis=1, keepdims=True)
        codes = codes + jnp.where(lane == k, tile_of, 0.0)
        codes = codes + jnp.where(lane == CAP + k, block_of, 0.0)
    out[pl.ds(2 * CAP, PEERS, stride=RECORD_ROWS), :] = codes


def pack(feats, owner, src, slot, dst, w_first, w_second):
    return pl.pallas_call(
        pack_kernel,
        out_shape=jax.ShapeDtypeStruct((PEERS * RECORD_ROWS, TILE), F32),
        name="pack",
    )(feats, owner, src, slot, dst, w_first, w_second)


RECORDS = FEAT * CAP * PEERS
OUTER = 4 * BAND + 10


def kept_tile(i, s, earlier):
    inner, outer = i - 4, 36 + i * (i + 1) // 2 + s - (8 - i)
    before = jnp.where(i >= 4, inner * BAND + s, jnp.where(s >= 8 - i, outer, -1))
    m = i - 4
    outer = 36 + m * (9 - m) // 2 + s
    after = jnp.where(i < 4, i * BAND + s, jnp.where(s <= 3 - m, outer, -1))
    return jnp.where(earlier, before, after)


def gather_kernel(scale, core, b0, b1, w_third, out, hid, code, spread):
    tiles = out.shape[0]
    rows_t = tiles * BPT
    for f in range(FEAT):
        blk = (b0, b1)[f // 2].at[pl.ds(f % 2 * PEERS * RECORD_ROWS, PEERS * RECORD_ROWS), :]
        codes = jnp.transpose(blk[pl.ds(2 * CAP, PEERS, stride=RECORD_ROWS), :]).astype(jnp.int32)
        for k in range(CAP):
            at = (f * CAP + k) * PEERS
            for half in range(2):
                hid[at : at + PEERS, half * TILE : (half + 1) * TILE] = blk[
                    pl.ds(2 * k + half, PEERS, stride=RECORD_ROWS), :
                ].astype(BF)
            tile_of, block_of = codes[k : k + 1, :], codes[CAP + k : CAP + k + 1, :]
            if tiles == OUTER:
                tile_of = kept_tile(tile_of // BAND, tile_of % BAND, core[0] == 0)
            place_of = (block_of % BPT) * rows_t + tile_of * BPT + block_of // BPT
            code[0:1, at : at + PEERS] = jnp.where(tile_of >= 0, place_of, -1)
    w = w_third[...].astype(F32)
    w = [
        jnp.concatenate(
            [w[:, g * 64 + h * COLS : g * 64 + (h + 1) * COLS] for g in range(FEAT)], axis=1
        )
        for h in range(2)
    ]

    def place(b, carry):
        turned = [pltpu.roll(x, 4 * b, 1).astype(BF) for x in w]
        spot = lax.broadcasted_iota(jnp.int32, (rows_t, RECORDS), 0) + b * rows_t
        onehot = jnp.where(spot == code[0:1, :], 1.0, 0.0).astype(BF)
        high, low = pieces(dot(onehot, hid[...]))
        turned = jnp.concatenate(turned, axis=1)
        spread[b] = (dot(high, turned) + dot(low, turned)) * scale
        return carry

    lax.fori_loop(0, BPT, place, 0)
    turn = (lax.broadcasted_iota(jnp.int32, (BPT, TILE), 1) // 4) % BPT

    def arrange(step, carry):
        for t in (2 * step, 2 * step + 1):
            rows = pl.ds(pl.multiple_of(t * BPT, BPT), BPT)
            for half in range(2):
                x = [
                    spread[(BPT - j) % BPT, rows, half * TILE : (half + 1) * TILE]
                    for j in range(BPT)
                ]
                for bit in (1, 2, 4):
                    moved = (turn // bit) % 2 == 1
                    x = [jnp.where(moved, x[(j - bit) % BPT], x[j]) for j in range(BPT)]
                for q in range(BPT):
                    comp = half * BPT + q
                    first = (comp // 4) * COLS + comp % 4
                    y = pltpu.roll(x[q], TILE - 4 * q, 1) if q else x[q]
                    out[t, pl.ds(first, BPT, stride=4), :] = y
        return carry

    lax.fori_loop(0, tiles // 2, arrange, 0)


def gather_blocks(scale, core, tiles, blocks, w):
    rows_t = tiles * BPT
    return pl.pallas_call(
        functools.partial(gather_kernel, scale),
        in_specs=[pl.BlockSpec(memory_space=pltpu.SMEM)]
        + [pl.BlockSpec(memory_space=pltpu.VMEM)] * 3,
        out_shape=jax.ShapeDtypeStruct((tiles, TILE, TILE), F32),
        scratch_shapes=[
            pltpu.VMEM((RECORDS, F), BF),
            pltpu.VMEM((8, RECORDS), jnp.int32),
            pltpu.VMEM((BPT, rows_t, F), F32),
        ],
        compiler_params=pltpu.CompilerParams(vmem_limit_bytes=24 * 2**20),
        cost_estimate=pl.CostEstimate(
            flops=2 * BPT * rows_t * F * (RECORDS + 2 * F),
            bytes_accessed=7 * 2**20,
            transcendentals=0,
        ),
        name="gather_blocks",
    )(core, *blocks, w)


PAIR = 2 * TILE
SPAN = 5 * PAIR
INNER = 8
SLICE = 2 * COLS


def purify_kernel(
    group, own_in, mine_in, other_in, out, own, sides, e_hi, e_lo, f_hi, f_lo, g_hi, g_lo, s_hi, s_lo, sems
):
    core = group[0] % 2
    copies = [
        pltpu.make_async_copy(own_in, own, sems.at[0]),
        pltpu.make_async_copy(mine_in, sides.at[core], sems.at[1]),
        pltpu.make_async_copy(other_in, sides.at[1 - core], sems.at[2]),
    ]
    for copy in copies:
        copy.start()

    def tile(a, s):
        if a < 4:
            return sides[0, 36 + a * (a + 1) // 2 + s - (8 - a)]
        if a < 8:
            return sides[0, (a - 4) * BAND + s]
        if a < 16:
            return own[(a - 8) * BAND + s]
        if a < 20:
            return sides[1, (a - 16) * BAND + s]
        return sides[1, 36 + (a - 20) * (29 - a) // 2 + s]

    def fill(inside):
        for a in range(4, 20):
            for s in range(BAND):
                b = a + s - HALF
                if inside == (8 <= a < 16 and 8 <= b < 16):
                    p, par = a // 2 - 2, a % 2
                    rows = slice(par * TILE, (par + 1) * TILE)
                    at = slice((s + par) * TILE, (s + par + 1) * TILE)
                    x = tile(a, s) + jnp.transpose(tile(b, BAND - 1 - s))
                    e_hi[p, rows, at], e_lo[p, rows, at] = pieces(x)

    zero = jnp.zeros((TILE, TILE), BF)
    for p in range(INNER):
        for rows, edge in ((slice(0, TILE), slice(9 * TILE, 10 * TILE)), (slice(TILE, PAIR), slice(0, TILE))):
            e_hi[p, rows, edge] = zero
            e_lo[p, rows, edge] = zero
    g_hi[...] = jnp.zeros_like(g_hi)
    g_lo[...] = jnp.zeros_like(g_lo)
    copies[0].wait()
    fill(True)
    copies[1].wait()
    copies[2].wait()
    fill(False)

    mine = pl.multiple_of(group[0] * COLS, COLS)
    row_tile = lax.broadcasted_iota(jnp.int32, (PAIR, PAIR), 0) // TILE
    col_tile = lax.broadcasted_iota(jnp.int32, (PAIR, PAIR), 1) // TILE

    def product(a_hi, a_lo, b_hi, b_lo):
        rows = a_hi.shape[0]
        both = dot_t(jnp.concatenate([a_hi, a_lo], axis=0), b_hi)
        return both[:rows] + (both[rows:] + dot_t(a_hi, b_lo))

    def square(d, p, carry):
        o = p + d
        k = SPAN - d * PAIR
        at = slice((2 + d) * PAIR, (3 + d) * PAIR)
        x = product(e_hi[p, :, d * PAIR :], e_lo[p, :, d * PAIR :], e_hi[o, :, :k], e_lo[o, :, :k])
        if d == 2:
            x = jnp.where(col_tile > row_tile, 0.0, x)
        x = x + (e_hi[p, :, at].astype(F32) + e_lo[p, :, at].astype(F32))
        f_hi[p, :, at], f_lo[p, :, at] = pieces(x)
        if d:
            back = slice((2 - d) * PAIR, (3 - d) * PAIR)
            f_hi[o, :, back], f_lo[o, :, back] = pieces(jnp.transpose(x))
        return carry

    for d, first in ((0, 2), (1, 1), (2, 0)):
        lax.fori_loop(first, 6, functools.partial(square, d), 0)

    for p in range(INNER):
        outside = (0, 1) if p < 2 else (6, 7) if p > 5 else ()
        others = [o for o in range(max(0, p - 2), min(INNER, p + 3)) if o not in outside]
        low, high = others[0], others[-1] + 1
        source = slice((low - p + 2) * PAIR, (high - p + 2) * PAIR)
        for par in range(2):
            from_rows = pl.ds(par * TILE + mine, COLS)
            to_rows = slice(p * SLICE + par * COLS, p * SLICE + (par + 1) * COLS)
            for g_ref, f_ref in ((g_hi, f_hi), (g_lo, f_lo)):
                g_ref[to_rows, low * PAIR : high * PAIR] = f_ref[p, from_rows, source]
    for base in (0, 6):
        s_hi[...] = jnp.zeros_like(s_hi)
        s_lo[...] = jnp.zeros_like(s_lo)
        for i in range(2):
            for par in range(2):
                from_rows = pl.ds(par * TILE + mine, COLS)
                to_rows = slice(i * SLICE + par * COLS, i * SLICE + (par + 1) * COLS)
                for s_ref, e_ref in ((s_hi, e_hi), (s_lo, e_lo)):
                    s_ref[to_rows, i * PAIR : i * PAIR + SPAN] = e_ref[base + i, from_rows, :]
        for i in range(2):
            o = base + i
            span = slice(i * PAIR, i * PAIR + SPAN)
            x = product(s_hi[:, span], s_lo[:, span], e_hi[o], e_lo[o])
            at = slice((i + 2) * PAIR, (i + 3) * PAIR)
            x = x + (s_hi[:, at].astype(F32) + s_lo[:, at].astype(F32))
            rows = slice(base * SLICE, (base + 2) * SLICE)
            g_hi[rows, o * PAIR : (o + 1) * PAIR], g_lo[rows, o * PAIR : (o + 1) * PAIR] = pieces(x)

    diagonal = lax.broadcasted_iota(jnp.int32, (COLS, TILE), 0) + mine == (
        lax.broadcasted_iota(jnp.int32, (COLS, TILE), 1)
    )
    diagonal = jnp.where(diagonal, 7.0 / 16.0, 0.0)
    for m in range(4):
        p = m + 2
        rows = slice(m * SLICE, (m + 5) * SLICE)
        span = slice(m * PAIR, (m + 5) * PAIR)
        at = slice(p * PAIR, (p + 1) * PAIR)
        x = product(g_hi[rows, span], g_lo[rows, span], f_hi[p], f_lo[p])
        x = 1.5 * (g_hi[rows, at].astype(F32) + g_lo[rows, at].astype(F32)) - x
        for par in range(2):
            for s in range(BAND):
                y = x[(s + par) * COLS : (s + par + 1) * COLS, par * TILE : (par + 1) * TILE]
                if s == HALF:
                    y = y + diagonal
                out[2 * m + par, s] = y


def purify(group, own, mine, other):
    return pl.pallas_call(
        purify_kernel,
        out_shape=jax.ShapeDtypeStruct((TILE_DEV, BAND, COLS, TILE), F32),
        in_specs=[pl.BlockSpec(memory_space=pltpu.SMEM)]
        + [pl.BlockSpec(memory_space=pl.ANY)] * 3,
        scratch_shapes=[
            pltpu.VMEM((TILE_DEV * BAND, TILE, TILE), F32),
            pltpu.VMEM((2, OUTER, TILE, TILE), F32),
        ]
        + [pltpu.VMEM((INNER, PAIR, SPAN), BF)] * 4
        + [pltpu.VMEM((INNER * SLICE, INNER * PAIR), BF)] * 2
        + [pltpu.VMEM((2 * SLICE, SPAN + PAIR), BF)] * 2
        + [pltpu.SemaphoreType.DMA((3,))],
        compiler_params=pltpu.CompilerParams(vmem_limit_bytes=42 * 2**20),
        name="purify",
    )(group, own, mine, other)


def swap(x, axis_bit):
    pairs = [(r * FEAT + g, r * FEAT + (g ^ axis_bit)) for r in range(PEERS) for g in range(FEAT)]
    return lax.ppermute(x, ("rows", "feat"), pairs)


def to_neighbour(x, same_core):
    count = PEERS * FEAT
    pairs = []
    for d in range(count):
        core = d % 2 if same_core else 1 - d % 2
        step = FEAT if core == 0 else -FEAT
        pairs.append((d, (d - d % 2 + core + step) % count))
    return lax.ppermute(x, ("rows", "feat"), pairs)


def local(edge_feats, edge_owner, src_local, band_slot, dst_local, w_first, w_second, w_third):
    edges = edge_feats.shape[0]
    row = lambda x: x.reshape(1, edges)
    sent = pack(
        edge_feats, row(edge_owner), row(src_local), row(band_slot), row(dst_local),
        w_first, w_second,
    )
    got = lax.all_to_all(
        sent.reshape(PEERS, 1, RECORD_ROWS * TILE), "rows", split_axis=0, concat_axis=0, tiled=True
    )
    got = got.reshape(PEERS * RECORD_ROWS, TILE)
    half_scale = 0.25 / math.sqrt(2.0 * BLOCK * FEAT * edges / (TILE_DEV * BPT))
    held = jnp.concatenate([got, swap(got, 2)], axis=0)
    near = [to_neighbour(held, True), to_neighbour(held, False)]
    group = lax.axis_index("feat").astype(jnp.int32).reshape(1)
    core = group % 2
    own = gather_blocks(half_scale, core, TILE_DEV * BAND, (held, swap(held, 1)), w_third)
    near, own = lax.optimization_barrier((near, own))
    mine = gather_blocks(half_scale, core, OUTER, near, w_third)
    return purify(group, own, mine, swap(mine, 1))


def solution(mesh):
    in_specs = (
        P(("rows", "feat"), None),
        P(("rows", "feat"), None),
        P(("rows", "feat")),
        P(("rows", "feat")),
        P(("rows", "feat")),
        P(),
        P(),
        P(),
    )
    out_specs = P("rows", None, "feat", None)
    return jax.shard_map(local, mesh=mesh, in_specs=in_specs, out_specs=out_specs, check_vma=False)
```

```python
import functools
import math

import jax
import jax.numpy as jnp
from jax import lax
from jax.experimental import pallas as pl
from jax.experimental.pallas import tpu as pltpu
from jax.sharding import PartitionSpec as P

BLOCK = 16
TILE = 128
BAND = 9
HALF = BAND // 2
TILE_DEV = 8
BPT = TILE // BLOCK
F = 256
CAP = 4
PEERS = 128
RECORD_ROWS = 2 * CAP + 1
FEAT = 4
COLS = TILE // FEAT
BF = jnp.bfloat16
F32 = jnp.float32


def dot(a, b):
    return jnp.dot(a, b, preferred_element_type=F32)


def dot_t(a, b):
    return lax.dot_general(a, b, (((1,), (1,)), ((), ())), preferred_element_type=F32)


def pieces(x):
    high = x.astype(BF)
    return high, (x - high.astype(F32)).astype(BF)


def pack_kernel(feats, owner, src, slot, dst, w_first, w_second, out):
    edges = feats.shape[0]
    hidden = jax.nn.silu(dot(feats[...], w_first[...])).astype(BF)
    hidden = jax.nn.silu(dot(hidden, w_second[...])).astype(BF)
    named = lax.broadcasted_iota(jnp.int32, (PEERS, edges), 0) == owner[...]
    onehot = named.astype(F32)
    before = lax.broadcasted_iota(jnp.int32, (edges, edges), 0) < lax.broadcasted_iota(
        jnp.int32, (edges, edges), 1
    )
    earlier = dot(onehot.astype(BF), before.astype(F32).astype(BF))
    rank = jnp.sum(onehot * earlier, axis=0, keepdims=True)
    src_v, slot_v, dst_v = src[...], slot[...], dst[...]
    tile_code = ((src_v // BPT) * BAND + slot_v).astype(F32)
    block_code = ((src_v % BPT) * BPT + dst_v).astype(F32)
    lane = lax.broadcasted_iota(jnp.int32, (PEERS, TILE), 1)
    codes = jnp.zeros((PEERS, TILE), F32)
    for k in range(CAP):
        chosen = jnp.where(rank == float(k), onehot, 0.0)
        placed = dot(chosen.astype(BF), hidden)
        out[pl.ds(2 * k, PEERS, stride=RECORD_ROWS), :] = placed[:, :TILE]
        out[pl.ds(2 * k + 1, PEERS, stride=RECORD_ROWS), :] = placed[:, TILE:]
        tile_of = jnp.sum(chosen * tile_code, axis=1, keepdims=True)
        block_of = jnp.sum(chosen * block_code, axis=1, keepdims=True)
        codes = codes + jnp.where(lane == k, tile_of, 0.0)
        codes = codes + jnp.where(lane == CAP + k, block_of, 0.0)
    out[pl.ds(2 * CAP, PEERS, stride=RECORD_ROWS), :] = codes


def pack(feats, owner, src, slot, dst, w_first, w_second):
    return pl.pallas_call(
        pack_kernel,
        out_shape=jax.ShapeDtypeStruct((PEERS * RECORD_ROWS, TILE), F32),
        name="pack",
    )(feats, owner, src, slot, dst, w_first, w_second)


RECORDS = FEAT * CAP * PEERS
OUTER = 4 * BAND + 10


DATA = 2 * CAP * PEERS


def join_kernel(a, b, out):
    for f, blk in enumerate((a, b)):
        for k in range(2 * CAP):
            row = f * DATA + k * PEERS
            out[row : row + PEERS, :] = blk[pl.ds(k, PEERS, stride=RECORD_ROWS), :]
        codes = jnp.transpose(blk[pl.ds(2 * CAP, PEERS, stride=RECORD_ROWS), :])
        out[2 * DATA + f * 8 : 2 * DATA + f * 8 + 8, :] = codes[:8, :]


def join(a, b):
    return pl.pallas_call(
        join_kernel,
        out_shape=jax.ShapeDtypeStruct((2 * DATA + 16, TILE), F32),
        compiler_params=pltpu.CompilerParams(vmem_limit_bytes=8 * 2**20),
        name="join",
    )(a, b)


def kept_tile(i, s, earlier):
    inner, outer = i - 4, 36 + i * (i + 1) // 2 + s - (8 - i)
    before = jnp.where(i >= 4, inner * BAND + s, jnp.where(s >= 8 - i, outer, -1))
    m = i - 4
    outer = 36 + m * (9 - m) // 2 + s
    after = jnp.where(i < 4, i * BAND + s, jnp.where(s <= 3 - m, outer, -1))
    return jnp.where(earlier, before, after)


def gather_kernel(scale, core, b0, b1, w_third, out, hid, code, spread):
    tiles = out.shape[0]
    rows_t = tiles * BPT
    for f in range(FEAT):
        blk, base = (b0, b1)[f // 2], f % 2 * DATA
        codes = blk[2 * DATA + f % 2 * 8 : 2 * DATA + f % 2 * 8 + 8, :].astype(jnp.int32)
        for k in range(CAP):
            at = (f * CAP + k) * PEERS
            for half in range(2):
                row = base + (2 * k + half) * PEERS
                hid[at : at + PEERS, half * TILE : (half + 1) * TILE] = blk[
                    row : row + PEERS, :
                ].astype(BF)
            tile_of, block_of = codes[k : k + 1, :], codes[CAP + k : CAP + k + 1, :]
            if tiles == OUTER:
                tile_of = kept_tile(tile_of // BAND, tile_of % BAND, core[0] == 0)
            place_of = (block_of % BPT) * rows_t + tile_of * BPT + block_of // BPT
            code[0:1, at : at + PEERS] = jnp.where(tile_of >= 0, place_of, -1)
    w = w_third[...].astype(F32)
    w = [
        jnp.concatenate(
            [w[:, g * 64 + h * COLS : g * 64 + (h + 1) * COLS] for g in range(FEAT)], axis=1
        )
        for h in range(2)
    ]

    def place(b, carry):
        turned = [pltpu.roll(x, 4 * b, 1).astype(BF) for x in w]
        spot = lax.broadcasted_iota(jnp.int32, (rows_t, RECORDS), 0) + b * rows_t
        onehot = jnp.where(spot == code[0:1, :], 1.0, 0.0).astype(BF)
        high, low = pieces(dot(onehot, hid[...]))
        turned = jnp.concatenate(turned, axis=1)
        spread[b] = (dot(high, turned) + dot(low, turned)) * scale
        return carry

    lax.fori_loop(0, BPT, place, 0)
    turn = (lax.broadcasted_iota(jnp.int32, (BPT, TILE), 1) // 4) % BPT

    def arrange(step, carry):
        for t in (2 * step, 2 * step + 1):
            rows = pl.ds(pl.multiple_of(t * BPT, BPT), BPT)
            for half in range(2):
                x = [
                    spread[(BPT - j) % BPT, rows, half * TILE : (half + 1) * TILE]
                    for j in range(BPT)
                ]
                for bit in (1, 2, 4):
                    moved = (turn // bit) % 2 == 1
                    x = [jnp.where(moved, x[(j - bit) % BPT], x[j]) for j in range(BPT)]
                for q in range(BPT):
                    comp = half * BPT + q
                    first = (comp // 4) * COLS + comp % 4
                    y = pltpu.roll(x[q], TILE - 4 * q, 1) if q else x[q]
                    out[t, pl.ds(first, BPT, stride=4), :] = y
        return carry

    lax.fori_loop(0, tiles // 2, arrange, 0)


def gather_blocks(scale, core, tiles, blocks, w):
    rows_t = tiles * BPT
    return pl.pallas_call(
        functools.partial(gather_kernel, scale),
        in_specs=[pl.BlockSpec(memory_space=pltpu.SMEM)]
        + [pl.BlockSpec(memory_space=pltpu.VMEM)] * 3,
        out_shape=jax.ShapeDtypeStruct((tiles, TILE, TILE), F32),
        scratch_shapes=[
            pltpu.VMEM((RECORDS, F), BF),
            pltpu.VMEM((8, RECORDS), jnp.int32),
            pltpu.VMEM((BPT, rows_t, F), F32),
        ],
        compiler_params=pltpu.CompilerParams(vmem_limit_bytes=24 * 2**20),
        cost_estimate=pl.CostEstimate(
            flops=2 * BPT * rows_t * F * (RECORDS + 2 * F),
            bytes_accessed=7 * 2**20,
            transcendentals=0,
        ),
        name="gather_blocks",
    )(core, *blocks, w)


PAIR = 2 * TILE
SPAN = 5 * PAIR
INNER = 8
SLICE = 2 * COLS


def purify_kernel(
    group, own_in, mine_in, other_in, out, own, sides, e_hi, e_lo, f_hi, f_lo, g_hi, g_lo, s_hi, s_lo, sems
):
    core = group[0] % 2
    copies = [
        pltpu.make_async_copy(own_in, own, sems.at[0]),
        pltpu.make_async_copy(mine_in, sides.at[core], sems.at[1]),
        pltpu.make_async_copy(other_in, sides.at[1 - core], sems.at[2]),
    ]
    for copy in copies:
        copy.start()

    def tile(a, s):
        if a < 4:
            return sides[0, 36 + a * (a + 1) // 2 + s - (8 - a)]
        if a < 8:
            return sides[0, (a - 4) * BAND + s]
        if a < 16:
            return own[(a - 8) * BAND + s]
        if a < 20:
            return sides[1, (a - 16) * BAND + s]
        return sides[1, 36 + (a - 20) * (29 - a) // 2 + s]

    def fill(inside):
        for a in range(4, 20):
            for s in range(BAND):
                b = a + s - HALF
                if inside == (8 <= a < 16 and 8 <= b < 16):
                    p, par = a // 2 - 2, a % 2
                    rows = slice(par * TILE, (par + 1) * TILE)
                    at = slice((s + par) * TILE, (s + par + 1) * TILE)
                    x = tile(a, s) + jnp.transpose(tile(b, BAND - 1 - s))
                    e_hi[p, rows, at], e_lo[p, rows, at] = pieces(x)

    zero = jnp.zeros((TILE, TILE), BF)
    for p in range(INNER):
        for rows, edge in ((slice(0, TILE), slice(9 * TILE, 10 * TILE)), (slice(TILE, PAIR), slice(0, TILE))):
            e_hi[p, rows, edge] = zero
            e_lo[p, rows, edge] = zero
    g_hi[...] = jnp.zeros_like(g_hi)
    g_lo[...] = jnp.zeros_like(g_lo)
    copies[0].wait()
    fill(True)
    copies[1].wait()
    copies[2].wait()
    fill(False)

    mine = pl.multiple_of(group[0] * COLS, COLS)
    row_tile = lax.broadcasted_iota(jnp.int32, (PAIR, PAIR), 0) // TILE
    col_tile = lax.broadcasted_iota(jnp.int32, (PAIR, PAIR), 1) // TILE

    def product(a_hi, a_lo, b_hi, b_lo):
        rows = a_hi.shape[0]
        both = dot_t(jnp.concatenate([a_hi, a_lo], axis=0), b_hi)
        return both[:rows] + (both[rows:] + dot_t(a_hi, b_lo))

    def square(d, p, carry):
        o = p + d
        k = SPAN - d * PAIR
        at = slice((2 + d) * PAIR, (3 + d) * PAIR)
        x = product(e_hi[p, :, d * PAIR :], e_lo[p, :, d * PAIR :], e_hi[o, :, :k], e_lo[o, :, :k])
        if d == 2:
            x = jnp.where(col_tile > row_tile, 0.0, x)
        x = x + (e_hi[p, :, at].astype(F32) + e_lo[p, :, at].astype(F32))
        f_hi[p, :, at], f_lo[p, :, at] = pieces(x)
        if d:
            back = slice((2 - d) * PAIR, (3 - d) * PAIR)
            f_hi[o, :, back], f_lo[o, :, back] = pieces(jnp.transpose(x))
        return carry

    for d, first in ((0, 2), (1, 1), (2, 0)):
        lax.fori_loop(first, 6, functools.partial(square, d), 0)

    for p in range(INNER):
        outside = (0, 1) if p < 2 else (6, 7) if p > 5 else ()
        others = [o for o in range(max(0, p - 2), min(INNER, p + 3)) if o not in outside]
        low, high = others[0], others[-1] + 1
        source = slice((low - p + 2) * PAIR, (high - p + 2) * PAIR)
        for par in range(2):
            from_rows = pl.ds(par * TILE + mine, COLS)
            to_rows = slice(p * SLICE + par * COLS, p * SLICE + (par + 1) * COLS)
            for g_ref, f_ref in ((g_hi, f_hi), (g_lo, f_lo)):
                g_ref[to_rows, low * PAIR : high * PAIR] = f_ref[p, from_rows, source]
    for base in (0, 6):
        s_hi[...] = jnp.zeros_like(s_hi)
        s_lo[...] = jnp.zeros_like(s_lo)
        for i in range(2):
            for par in range(2):
                from_rows = pl.ds(par * TILE + mine, COLS)
                to_rows = slice(i * SLICE + par * COLS, i * SLICE + (par + 1) * COLS)
                for s_ref, e_ref in ((s_hi, e_hi), (s_lo, e_lo)):
                    s_ref[to_rows, i * PAIR : i * PAIR + SPAN] = e_ref[base + i, from_rows, :]
        for i in range(2):
            o = base + i
            span = slice(i * PAIR, i * PAIR + SPAN)
            x = product(s_hi[:, span], s_lo[:, span], e_hi[o], e_lo[o])
            at = slice((i + 2) * PAIR, (i + 3) * PAIR)
            x = x + (s_hi[:, at].astype(F32) + s_lo[:, at].astype(F32))
            rows = slice(base * SLICE, (base + 2) * SLICE)
            g_hi[rows, o * PAIR : (o + 1) * PAIR], g_lo[rows, o * PAIR : (o + 1) * PAIR] = pieces(x)

    diagonal = lax.broadcasted_iota(jnp.int32, (COLS, TILE), 0) + mine == (
        lax.broadcasted_iota(jnp.int32, (COLS, TILE), 1)
    )
    diagonal = jnp.where(diagonal, 7.0 / 16.0, 0.0)
    for m in range(4):
        p = m + 2
        rows = slice(m * SLICE, (m + 5) * SLICE)
        span = slice(m * PAIR, (m + 5) * PAIR)
        at = slice(p * PAIR, (p + 1) * PAIR)
        x = product(g_hi[rows, span], g_lo[rows, span], f_hi[p], f_lo[p])
        x = 1.5 * (g_hi[rows, at].astype(F32) + g_lo[rows, at].astype(F32)) - x
        for par in range(2):
            for s in range(BAND):
                y = x[(s + par) * COLS : (s + par + 1) * COLS, par * TILE : (par + 1) * TILE]
                if s == HALF:
                    y = y + diagonal
                out[2 * m + par, s] = y


def purify(group, own, mine, other):
    return pl.pallas_call(
        purify_kernel,
        out_shape=jax.ShapeDtypeStruct((TILE_DEV, BAND, COLS, TILE), F32),
        in_specs=[pl.BlockSpec(memory_space=pltpu.SMEM)]
        + [pl.BlockSpec(memory_space=pl.ANY)] * 3,
        scratch_shapes=[
            pltpu.VMEM((TILE_DEV * BAND, TILE, TILE), F32),
            pltpu.VMEM((2, OUTER, TILE, TILE), F32),
        ]
        + [pltpu.VMEM((INNER, PAIR, SPAN), BF)] * 4
        + [pltpu.VMEM((INNER * SLICE, INNER * PAIR), BF)] * 2
        + [pltpu.VMEM((2 * SLICE, SPAN + PAIR), BF)] * 2
        + [pltpu.SemaphoreType.DMA((3,))],
        compiler_params=pltpu.CompilerParams(vmem_limit_bytes=42 * 2**20),
        name="purify",
    )(group, own, mine, other)


def swap(x, axis_bit):
    pairs = [(r * FEAT + g, r * FEAT + (g ^ axis_bit)) for r in range(PEERS) for g in range(FEAT)]
    return lax.ppermute(x, ("rows", "feat"), pairs)


def to_neighbour(x, same_core):
    count = PEERS * FEAT
    pairs = []
    for d in range(count):
        core = d % 2 if same_core else 1 - d % 2
        step = FEAT if core == 0 else -FEAT
        pairs.append((d, (d - d % 2 + core + step) % count))
    return lax.ppermute(x, ("rows", "feat"), pairs)


def local(edge_feats, edge_owner, src_local, band_slot, dst_local, w_first, w_second, w_third):
    edges = edge_feats.shape[0]
    row = lambda x: x.reshape(1, edges)
    sent = pack(
        edge_feats, row(edge_owner), row(src_local), row(band_slot), row(dst_local),
        w_first, w_second,
    )
    got = lax.all_to_all(
        sent.reshape(PEERS, 1, RECORD_ROWS * TILE), "rows", split_axis=0, concat_axis=0, tiled=True
    )
    got = got.reshape(PEERS * RECORD_ROWS, TILE)
    half_scale = 0.25 / math.sqrt(2.0 * BLOCK * FEAT * edges / (TILE_DEV * BPT))
    held = join(got, swap(got, 2))
    near = [to_neighbour(held, True), to_neighbour(held, False)]
    group = lax.axis_index("feat").astype(jnp.int32).reshape(1)
    core = group % 2
    own = gather_blocks(half_scale, core, TILE_DEV * BAND, (held, swap(held, 1)), w_third)
    near, own = lax.optimization_barrier((near, own))
    mine = gather_blocks(half_scale, core, OUTER, near, w_third)
    return purify(group, own, mine, swap(mine, 1))


def solution(mesh):
    in_specs = (
        P(("rows", "feat"), None),
        P(("rows", "feat"), None),
        P(("rows", "feat")),
        P(("rows", "feat")),
        P(("rows", "feat")),
        P(),
        P(),
        P(),
    )
    out_specs = P("rows", None, "feat", None)
    return jax.shard_map(local, mesh=mesh, in_specs=in_specs, out_specs=out_specs, check_vma=False)
```
